128 devices in a mesh: row: 16 (over x_lo, y, core), col: 8 (over z, x_hi).
Axes of the slice: x: 4 (x_hi: 2, x_lo: 2; x = x_hi * 2 + x_lo), y: 4, z: 4, core: 2. Of those that a mesh axis runs over, the one named last changes fastest.
Arguments:
- ancestor: bfloat16 [16384, 16384], P('row', 'col'), as said below
- panels: bfloat16 [3, 8192, 256], P(None, ('row', 'col')), may hold values from -0.625 to 0.625
- row_index: int32 [3, 8192], P(None, ('row', 'col')), may hold values from 0 to 16383, as said below
- diag_inverse: float32 [3, 256, 256], replicated, may hold values from -6 to 6
Outputs:
- off_block: bfloat16 [16384, 768], P(('row', 'col'))
- diag_block: float32 [3, 256, 256], replicated
The draws below stay inside these ranges and needn't reach their ends.
Inputs may be any that keep to these rules, and one draw needn't show every extreme that they name: `row_index`: each of the 3 lists names 8192 different ancestor rows; row 0 and row 16383 are in every list. `ancestor`: entries on and below the diagonal are read; diagonal entries lie between 0.75 and 1.25 plus the off-diagonal spread.
All inputs are finite; a program needn't handle non-finite values.
Results may differ from the reference program's by a relative error of at most 0.014.
Values may be sent and summed in bfloat16 or wider, within the bound.
A program may use at most 64 MiB of HBM per device.

```python
import jax
import jax.numpy as jnp
from jax import lax

NA = 16384
W = 256
SIBS = 3
RS = 8192
N_ROW = 16
N_COL = 8


def draw_ancestor(key, part):
    key_noise = jax.random.fold_in(key, 0)
    key_diag = jax.random.fold_in(key, 2)
    noise_part = jax.random.normal(key_noise, (NA, NA), jnp.float32)
    matrix = noise_part * (2.0 * RS) ** (-0.5)
    diag_values = 1.0 + 0.25 * jax.random.uniform(key_diag, (NA,), jnp.float32, -1.0, 1.0)
    positions = jnp.arange(NA, dtype=jnp.int32)
    matrix = matrix.at[positions, positions].add(diag_values)
    return matrix.astype(jnp.bfloat16)


def draw_row_index(key, part):
    chosen_lists = []
    for sibling in range(SIBS):
        chosen = jax.random.permutation(jax.random.fold_in(key, 7 + sibling), NA - 2)[:RS - 2] + 1
        complete = jnp.concatenate([jnp.array([0, NA - 1], jnp.int32), chosen.astype(jnp.int32)])
        shuffle_order = jax.random.permutation(jax.random.fold_in(key, 101 + sibling), RS)
        chosen_lists.append(complete[shuffle_order])
    return jnp.stack(chosen_lists).astype(jnp.int32)


def steps_of(rng, shape, cuts, smallest, largest):
    def one(dim, shards_of):
        draws = jax.random.uniform(jax.random.fold_in(jax.random.fold_in(rng, 6), dim), (shards_of,), jnp.float32, smallest / len(cuts), largest / len(cuts))
        return jnp.repeat(jnp.exp(draws), shape[dim] // shards_of).reshape((-1,) + (1,) * (len(shape) - dim - 1))

    loudness = one(*cuts[0])
    for cut in cuts[1:]:
        loudness = loudness * one(*cut)
    return loudness


def gaussian(own_key, dims, width, limit, pieces=(), held_as=jnp.bfloat16):
    result = width * jax.random.normal(own_key, dims, jnp.float32)
    if pieces:
        result = result * steps_of(own_key, dims, pieces, -0.22, 0.18)
    return jnp.clip(result, -limit, limit).astype(held_as)


def setup_inputs(seed: int = 0) -> dict:
    splits = jax.random.split(jax.random.key(seed), 5)
    return {
        "ancestor": draw_ancestor(jax.random.fold_in(splits[4], 71), 0),
        "panels": gaussian(splits[1], (SIBS, RS, W), (4 * RS ** -0.5), 0.625, ((1, 128),)),
        "row_index": draw_row_index(jax.random.fold_in(splits[4], 71), 0),
        "diag_inverse": gaussian(splits[3], (SIBS, W, W), 1.0, 6.0, (), jnp.float32),
    }


def reference(ancestor, panels, row_index, diag_inverse):
    features = SIBS * W
    sibling = jnp.broadcast_to(jnp.arange(SIBS, dtype=jnp.int32)[:, None], row_index.shape)
    spread = jnp.zeros((NA, SIBS, W), jnp.bfloat16).at[row_index, sibling].set(panels)
    member = jnp.zeros((NA, SIBS), jnp.float32).at[row_index, sibling].set(1.0)
    spread_flat = spread.reshape(NA, features)
    block_rows = NA // N_ROW
    block_cols = NA // N_COL
    col_blocks = spread_flat.reshape(N_COL, block_cols, features).astype(jnp.float32)

    def row_block(mirror_sum, block_index):
        first_row = block_index * block_rows
        rows_part = lax.dynamic_slice_in_dim(ancestor, first_row, block_rows, 0)
        row_ids = first_row + lax.broadcasted_iota(jnp.int32, (block_rows, NA), 0)
        col_ids = lax.broadcasted_iota(jnp.int32, (block_rows, NA), 1)
        lower_part = jnp.where(col_ids <= row_ids, rows_part, 0).astype(jnp.float32)
        lower_part = lower_part.reshape(block_rows, N_COL, block_cols)
        strict = jnp.where(col_ids < row_ids, rows_part, 0).astype(jnp.float32)
        strict = strict.reshape(block_rows, N_COL, block_cols)
        direct = jnp.einsum("rcx,cxk->crk", lower_part, col_blocks, precision=lax.Precision.HIGHEST)
        direct = lax.optimization_barrier(direct.astype(jnp.bfloat16)).astype(jnp.float32)
        direct = jnp.sum(direct, axis=0)
        own_spread = lax.dynamic_slice_in_dim(spread_flat, first_row, block_rows, 0).astype(jnp.float32)
        mirrored = jnp.einsum("rcx,rk->cxk", strict, own_spread, precision=lax.Precision.HIGHEST)
        mirrored = lax.optimization_barrier(mirrored.astype(jnp.bfloat16)).astype(jnp.float32)
        return mirror_sum + mirrored.reshape(NA, features), direct

    mirror_sum, direct_rows = lax.scan(row_block, jnp.zeros((NA, features), jnp.float32), jnp.arange(N_ROW, dtype=jnp.int32))
    product = direct_rows.reshape(NA, features) + mirror_sum
    product3 = product.reshape(NA, SIBS, W)
    off_block = jnp.where(member[:, :, None] > 0.5, -product3, 0.0).astype(jnp.bfloat16).reshape(NA, features)
    diag_block = diag_inverse + jnp.einsum("asw,asv->swv", spread.astype(jnp.float32), product3, precision=lax.Precision.HIGHEST)
    return off_block, diag_block
```

```python
import jax
import jax.numpy as jnp
from jax import lax
from jax.experimental import pallas as pl
from jax.experimental.pallas import tpu as pltpu
from jax.sharding import PartitionSpec as P

MESH = pl.DeviceIdType.MESH
F32 = jnp.float32
BF16 = jnp.bfloat16
N_SEM = 192
G_ROWS = 16


def mod(value, size):
    return lax.rem(value + 2 * size, size)


def kernel(
    anc_ref, pan_ref, idx_ref, dinv_ref, off_ref, diag_ref,
    a_buf, at_buf, g_buf, i_buf, i_far, acc, px_send, px_recv, s_row, s_col, member,
    d_val, d_half, m_val, m_half, g_val, d1s, d1r, d2s, d2r, d3s, d3r,
    mcs, mcr, m1s, m1r, m2s, m2r, m3s, m3r, mts, mtr,
    gcs, gcr, g1s, g1r, g2s, g2r, g3s, g3r, grow, gcol,
    send_sem, recv_sem, load_sem,
):
    row = lax.axis_index("row")
    col = lax.axis_index("col")
    core = lax.rem(row, 2)
    y = lax.rem(lax.div(row, 2), 4)
    x_lo = lax.div(row, 8)
    x_hi = lax.rem(col, 2)
    z = lax.div(col, 2)
    x = x_hi * 2 + x_lo
    pair = lax.div(row, 2)
    where = {"x": x, "y": y, "z": z}

    def device(px, py, pz, pc):
        return (lax.rem(px, 2) * 8 + py * 2 + pc, pz * 2 + lax.div(px, 2))

    def neighbour(axis, step):
        place = dict(where)
        place[axis] = mod(place[axis] + step, 4)
        return device(place["x"], place["y"], place["z"], core)

    partner = (row + 1 - 2 * core, col)
    x_far = (row, col + 1 - 2 * x_hi)
    x_near = (row + 8 - 16 * x_lo, col)
    row_far = row + 8 - 16 * x_lo
    col_far = col + 1 - 2 * x_hi
    turn_to = (2 * col + x_lo, y * 2 + core)
    turn_from = (lax.rem(row, 2) * 8 + col, lax.div(row, 2))
    fixed = (turn_to[0] == row) & (turn_to[1] == col)

    used = [0]
    copies = []

    def remote(src, dst, dev):
        n = used[0]
        used[0] += 1
        copy = pltpu.make_async_remote_copy(
            src_ref=src, dst_ref=dst, send_sem=send_sem.at[n], recv_sem=recv_sem.at[n],
            device_id=dev, device_id_type=MESH,
        )
        copies.append(copy)
        return copy

    def send(src, dst, dev):
        copy = remote(src, dst, dev)
        copy.start()
        return copy

    load_a = pltpu.make_async_copy(anc_ref, a_buf, load_sem.at[0])
    load_a.start()
    orders = (("x", "y", "z"), ("y", "z", "x"), ("z", "x", "y"))
    loads = []
    for s, (ra, rb, rc) in enumerate(orders):
        loads.append(
            pltpu.make_async_copy(
                pan_ref.at[s], g_buf.at[s, where[rc], where[rb], where[ra]], load_sem.at[1 + s]
            )
        )
    loads.append(pltpu.make_async_copy(idx_ref, i_buf.at[z, y, x], load_sem.at[4]))
    for one in loads:
        one.start()

    barrier = pltpu.get_barrier_semaphore()

    def greet(dev):
        pl.semaphore_signal(barrier, inc=1, device_id=dev, device_id_type=MESH)

    for step in (1, 3):
        greet(neighbour("x", step))
    for step in range(1, 16):
        greet((mod(row + step, 16), col))
    for step in range(1, 8):
        greet((row, mod(col + step, 8)))

    @pl.when(jnp.logical_not(fixed))
    def _():
        greet(turn_to)

    pl.semaphore_wait(barrier, jnp.where(fixed, 24, 25))

    for one in loads:
        one.wait()

    def gather(axis, whole, half):
        here = where[axis]
        plus, minus = neighbour(axis, 1), neighbour(axis, 3)
        before, after = mod(here + 3, 4), mod(here + 1, 4)
        up = send(whole(here), whole(here), plus)
        down = send(whole(here), whole(here), minus)
        yield
        up.wait_recv()
        up2 = send(half(before, 0), half(before, 0), plus)
        down.wait_recv()
        down2 = send(half(after, 1), half(after, 1), minus)
        yield
        up2.wait_recv()
        down2.wait_recv()
        yield

    def run(*paths):
        for path in paths:
            next(path)

    chains = []
    for s, (ra, rb, rc) in enumerate(orders):
        ma, mb, mc = where[ra], where[rb], where[rc]
        g = g_buf.at[s]
        chains.append(
            dict(
                a=gather(ra, lambda i, g=g, mc=mc, mb=mb: g.at[mc, mb, i],
                         lambda i, h, g=g, mc=mc, mb=mb: g.at[mc, mb, i, pl.ds(32 * h, 32)]),
                b=gather(rb, lambda i, g=g, mc=mc: g.at[mc, i],
                         lambda i, h, g=g, mc=mc: g.at[mc, i, pl.ds(2 * h, 2)]),
                c=[
                    gather(rc, lambda i, g=g, j=mod(mb + o, 4): g.at[i, j],
                           lambda i, h, g=g, j=mod(mb + o, 4): g.at[i, j, pl.ds(2 * h, 2)])
                    for o in (0, 3, 1, 2)
                ],
                planes=[mc, mod(mc + 3, 4), mod(mc + 1, 4), mod(mc + 2, 4)],
            )
        )
    ia = gather("x", lambda i: i_buf.at[z, y, i], lambda i, h: i_buf.at[z, y, i, pl.ds(2 * h, 2)])
    ib = gather("y", lambda i: i_buf.at[z, i], lambda i, h: i_buf.at[z, i, pl.ds(2 * h, 2)])
    ic = gather("z", lambda i: i_buf.at[i], lambda i, h: i_buf.at[i, pl.ds(2 * h, 2)])

    all_a = [ia] + [c["a"] for c in chains]
    all_b = [ib] + [c["b"] for c in chains]
    run(*all_a)
    run(*all_a)
    for n in range(4):
        run(all_a[n], all_b[n])
        if n:
            run(chains[n - 1]["c"][0])
    for n in range(4):
        run(all_b[n])
        if n:
            run(chains[n - 1]["c"][1], chains[n - 1]["c"][2])
    for c in chains:
        run(c["c"][0])
    for n in range(4):
        run(all_b[n])
        if n:
            run(chains[n - 1]["c"][3])
    run(ic)
    for c in chains:
        run(c["c"][1], c["c"][2])
    run(ic)
    run(ic)

    load_a.wait()

    row_start = row * 1024
    col_start = col * 2048

    def mask(i, _):
        r0 = pl.multiple_of(i * 128, 128)
        val = a_buf[pl.ds(r0, 128), :].astype(F32)
        gap = (
            lax.broadcasted_iota(jnp.int32, (128, 2048), 1)
            - lax.broadcasted_iota(jnp.int32, (128, 2048), 0)
            + (col_start - row_start - i * 128)
        )
        a_buf[pl.ds(r0, 128), :] = jnp.where(gap <= 0, val, 0.0).astype(BF16)
        at_buf[:, pl.ds(r0, 128)] = jnp.where(gap < 0, val, 0.0).T.astype(BF16)
        return 0

    def plane_dot(s, cc, first):
        ra, rb, rc = orders[s]
        lane = lax.broadcasted_iota(jnp.int32, (1, 128), 1)
        pieces = []
        for cb in range(4):
            for ca in (0, 2):
                pos = {rc: cc, rb: cb, ra: ca}
                pos2 = {rc: cc, rb: cb, ra: ca + 1}
                left = i_buf[pos["z"], pos["y"], pos["x"], pl.ds(s, 1), :]
                right = i_buf[pos2["z"], pos2["y"], pos2["x"], pl.ds(s, 1), :]
                pieces.append(jnp.where(lane < 64, left, right))

        def block(j, _):
            k = lax.div(j, 2)
            t = lax.rem(j, 2)
            base = jnp.where(
                t == 0, (2 * pair + k) * 1024 + col * 128, col * 2048 + (2 * pair + k) * 128
            )
            target = lax.broadcasted_iota(jnp.int32, (128, 128), 0) + base
            hot = jnp.concatenate(
                [jnp.where(target == piece, 1.0, 0.0).astype(BF16) for piece in pieces], axis=1
            )
            out = jnp.dot(hot, g_buf[s, cc].reshape(1024, 256), preferred_element_type=F32)
            cols = pl.ds(s * 256, 256)
            if first:
                acc[j, :, cols] = out
            else:
                acc[j, :, cols] = acc[j, :, cols] + out
            return 0

        lax.fori_loop(0, 4, block, 0)

    for s, c in enumerate(chains):
        plane_dot(s, c["planes"][0], True)
        run(chains[s]["c"][0])
        run(chains[s]["c"][3])
    lax.fori_loop(0, 8, mask, 0)
    for s, c in enumerate(chains):
        run(c["c"][1], c["c"][2])
        plane_dot(s, c["planes"][1], False)
        plane_dot(s, c["planes"][2], False)
    for s, c in enumerate(chains):
        run(c["c"][3])
        plane_dot(s, c["planes"][3], False)

    px_send[...] = acc[pl.ds(2 - 2 * core, 2)].astype(BF16)
    swap = send(px_send, px_recv, partner)
    swap_i = send(i_buf, i_far, partner)
    swap.wait_recv()
    s_row[col] = (acc[2 * core] + px_recv[0].astype(F32)).astype(BF16)
    s_col[row] = (acc[2 * core + 1] + px_recv[1].astype(F32)).astype(BF16)

    def half_rows(ref):
        return lambda i, h: ref(i).at[pl.ds(64 * h, 64)]

    def row_slot(hi):
        return lambda i: s_row.at[i * 2 + hi]

    def col_slot(lo):
        return lambda i: s_col.at[lo * 8 + i * 2 + core]

    x_row = send(s_row.at[col], s_row.at[col], x_far)
    x_col = send(s_col.at[row], s_col.at[row], x_near)
    z_own = gather("z", row_slot(x_hi), half_rows(row_slot(x_hi)))
    y_own = gather("y", col_slot(x_lo), half_rows(col_slot(x_lo)))
    z_far = gather("z", row_slot(1 - x_hi), half_rows(row_slot(1 - x_hi)))
    y_far = gather("y", col_slot(1 - x_lo), half_rows(col_slot(1 - x_lo)))
    across = []

    def cross(lo, i):
        ref = col_slot(lo)(i)
        across.append(send(ref, ref, partner))

    run(y_own, z_own)
    cross(x_lo, y)
    x_col.wait_recv()
    run(y_far)
    cross(1 - x_lo, y)
    x_row.wait_recv()
    run(z_far)
    run(y_own, z_own)
    cross(x_lo, mod(y + 1, 4))
    cross(x_lo, mod(y + 3, 4))
    run(y_far, z_far)
    cross(1 - x_lo, mod(y + 1, 4))
    cross(1 - x_lo, mod(y + 3, 4))

    swap_i.wait_recv()
    lane = lax.broadcasted_iota(jnp.int32, (1, 128), 1)
    own_rows = lax.broadcasted_iota(jnp.int32, (128, 128), 0) + (row * 1024 + col * 128)
    for s in range(3):
        def seen(n, found, s=s):
            pz, py = lax.div(n, 4), lax.rem(n, 4)
            for buf in (i_buf, i_far):
                for px in (0, 2):
                    left = buf[pz, py, px, pl.ds(s, 1), :]
                    right = buf[pz, py, px + 1, pl.ds(s, 1), :]
                    line = jnp.where(lane < 64, left, right)
                    found = jnp.where(own_rows == line, 1.0, found)
            return found
        found = lax.fori_loop(0, 16, seen, jnp.zeros((128, 128), F32))
        flag = jnp.max(found, axis=1, keepdims=True)
        member[:, pl.ds(s * 256, 256)] = jnp.broadcast_to(flag, (128, 256))

    run(y_own, z_own)
    cross(x_lo, mod(y + 2, 4))
    run(y_far, z_far)
    cross(1 - x_lo, mod(y + 2, 4))

    def mirrored(i, _):
        r0 = pl.multiple_of(i * 256, 256)
        out = jnp.dot(
            at_buf[pl.ds(r0, 256), :], s_row[...].reshape(1024, 768), preferred_element_type=F32
        )
        m_val[i] = out.reshape(2, 128, 768)
        m_half[pl.ds(r0, 256), :] = out.astype(BF16)
        return 0

    lax.fori_loop(0, 8, mirrored, 0)
    for one in across:
        one.wait_recv()

    def reduce_column(own, cs, cr, r1s, r1r, r2s, r2r, r3s, r3r):
        for i in range(8):
            cs[i] = own[i, 1 - core].astype(BF16)
        c0 = send(cs, cr, partner)
        yield
        c0.wait_recv()

        def val(lo, i):
            n = lo * 4 + i
            return own[n, core] + cr[n].astype(F32)

        plus, minus = neighbour("y", 1), neighbour("y", 3)
        y1, y2, y3 = mod(y + 1, 4), mod(y + 2, 4), mod(y + 3, 4)
        r1s[0] = val(0, y2).astype(BF16)
        p1 = send(r1s.at[0], r1r.at[0], plus)
        r1s[1] = val(1, y2).astype(BF16)
        n1 = send(r1s.at[1], r1r.at[1], minus)
        r2s[0, 1] = val(1, y1).astype(BF16)
        p2b = send(r2s.at[0, 1], r2r.at[0, 1], plus)
        r2s[1, 0] = val(0, y3).astype(BF16)
        n2a = send(r2s.at[1, 0], r2r.at[1, 0], minus)
        yield
        p1.wait_recv()
        r2s[0, 0] = (val(0, y1) + r1r[0].astype(F32)).astype(BF16)
        p2a = send(r2s.at[0, 0], r2r.at[0, 0], plus)
        n1.wait_recv()
        r2s[1, 1] = (val(1, y3) + r1r[1].astype(F32)).astype(BF16)
        n2b = send(r2s.at[1, 1], r2r.at[1, 1], minus)
        yield
        for one in (p2b, n2a, p2a, n2b):
            one.wait_recv()

        def total(lo):
            return val(lo, y) + r2r[0, lo].astype(F32) + r2r[1, lo].astype(F32)

        r3s[...] = total(1 - x_lo).astype(BF16)
        e = send(r3s, r3r, x_near)
        yield
        e.wait_recv()
        yield total(x_lo) + r3r[...].astype(F32)

    def reduce_row():
        plus, minus = neighbour("z", 1), neighbour("z", 3)
        z1, z2, z3 = mod(z + 1, 4), mod(z + 2, 4), mod(z + 3, 4)
        d1s[0] = d_val[z2 * 2].astype(BF16)
        p1 = send(d1s.at[0], d1r.at[0], plus)
        d1s[1] = d_val[z2 * 2 + 1].astype(BF16)
        n1 = send(d1s.at[1], d1r.at[1], minus)
        d2s[0, 1] = d_val[z1 * 2 + 1].astype(BF16)
        p2b = send(d2s.at[0, 1], d2r.at[0, 1], plus)
        d2s[1, 0] = d_val[z3 * 2].astype(BF16)
        n2a = send(d2s.at[1, 0], d2r.at[1, 0], minus)
        yield
        p1.wait_recv()
        d2s[0, 0] = (d_val[z1 * 2] + d1r[0].astype(F32)).astype(BF16)
        p2a = send(d2s.at[0, 0], d2r.at[0, 0], plus)
        n1.wait_recv()
        d2s[1, 1] = (d_val[z3 * 2 + 1] + d1r[1].astype(F32)).astype(BF16)
        n2b = send(d2s.at[1, 1], d2r.at[1, 1], minus)
        yield
        for one in (p2b, n2a, p2a, n2b):
            one.wait_recv()

        def total(hi):
            return d_val[z * 2 + hi] + d2r[0, hi].astype(F32) + d2r[1, hi].astype(F32)

        d3s[...] = total(1 - x_hi).astype(BF16)
        e = send(d3s, d3r, x_far)
        yield
        e.wait_recv()
        yield total(x_hi) + d3r[...].astype(F32)

    m_path = reduce_column(m_val, mcs, mcr, m1s, m1r, m2s, m2r, m3s, m3r)
    run(m_path)

    def direct(i):
        r0 = i * 256
        out = jnp.dot(
            a_buf[pl.ds(r0, 256), :], s_col[...].reshape(2048, 768), preferred_element_type=F32
        )
        d_val[pl.ds(2 * i, 2)] = out.reshape(2, 128, 768)
        d_half[pl.ds(r0, 256), :] = out.astype(BF16)

    lax.fori_loop(0, 2, lambda i, _: (direct(i), 0)[1], 0)
    run(m_path)
    lax.fori_loop(2, 4, lambda i, _: (direct(i), 0)[1], 0)
    d_path = reduce_row()
    run(d_path)
    run(m_path)

    along = (((0,), (0,)), ((), ()))
    for s in range(3):
        cols = pl.ds(s * 256, 256)
        out = lax.dot_general(
            s_row[:, :, cols].reshape(1024, 256), d_half[:, cols], along, preferred_element_type=F32
        ) + lax.dot_general(
            s_col[:, :, cols].reshape(2048, 256), m_half[:, cols], along, preferred_element_type=F32
        )
        g_val[:, :, :, cols] = out.reshape(8, 2, G_ROWS, 256)

    g_path = reduce_column(g_val, gcs, gcr, g1s, g1r, g2s, g2r, g3s, g3r)
    run(g_path)
    run(d_path)
    run(g_path)
    run(m_path)
    run(g_path)
    m_own = next(m_path)
    mts[...] = m_own.astype(BF16)

    turn = remote(mts, mtr, turn_to)

    @pl.when(jnp.logical_not(fixed))
    def _():
        turn.start()

    @pl.when(fixed)
    def _():
        mtr[...] = mts[...]

    run(d_path)
    run(g_path)
    grow[col] = next(g_path)
    row_sends = [
        send(grow.at[col], grow.at[col], (row, mod(col + step, 8))) for step in range(1, 8)
    ]
    d_own = next(d_path)

    @pl.when(jnp.logical_not(fixed))
    def _():
        turn.wait_recv()

    product = d_own + mtr[...].astype(F32)
    off_ref[...] = jnp.where(member[...] > 0.5, -product, 0.0).astype(BF16)

    for one in row_sends:
        one.wait_recv()
    total = grow[0]
    for n in range(1, 8):
        total = total + grow[n]
    gcol[row] = total
    col_sends = [
        send(gcol.at[row], gcol.at[row], (mod(row + step, 16), col)) for step in range(1, 16)
    ]
    for one in col_sends:
        one.wait_recv()
    for s in range(3):
        diag_ref[s] = dinv_ref[s] + gcol[:, :, pl.ds(s * 256, 256)].reshape(256, 256)

    for one in copies:
        if one is not turn:
            one.wait_send()

    @pl.when(jnp.logical_not(fixed))
    def _():
        turn.wait_send()


def per_device(ancestor, panels, row_index, diag_inverse):
    V = pltpu.VMEM
    lists = jnp.concatenate([row_index, row_index], axis=1)
    lists = jnp.concatenate([lists, lists[:1]], axis=0)
    any_spec = pl.BlockSpec(memory_space=pl.ANY)
    vmem_spec = pl.BlockSpec(memory_space=pltpu.VMEM)

    def ring(rows):
        return [
            V((8, rows, 768), BF16), V((8, rows, 768), BF16),
            V((2, rows, 768), BF16), V((2, rows, 768), BF16),
            V((2, 2, rows, 768), BF16), V((2, 2, rows, 768), BF16),
            V((rows, 768), BF16), V((rows, 768), BF16),
        ]

    scratch = [
        V((1024, 2048), BF16), V((2048, 1024), BF16),
        V((3, 4, 4, 4, 64, 256), BF16), V((4, 4, 4, 4, 128), jnp.int32),
        V((4, 4, 4, 4, 128), jnp.int32),
        V((4, 128, 768), F32), V((2, 128, 768), BF16), V((2, 128, 768), BF16),
        V((8, 128, 768), BF16), V((16, 128, 768), BF16), V((128, 768), F32),
        V((8, 128, 768), F32), V((1024, 768), BF16),
        V((8, 2, 128, 768), F32), V((2048, 768), BF16), V((8, 2, G_ROWS, 768), F32),
        V((2, 128, 768), BF16), V((2, 128, 768), BF16),
        V((2, 2, 128, 768), BF16), V((2, 2, 128, 768), BF16),
        V((128, 768), BF16), V((128, 768), BF16),
        *ring(128), V((128, 768), BF16), V((128, 768), BF16),
        *ring(G_ROWS), V((8, G_ROWS, 768), F32), V((16, G_ROWS, 768), F32),
        pltpu.SemaphoreType.DMA((N_SEM,)), pltpu.SemaphoreType.DMA((N_SEM,)),
        pltpu.SemaphoreType.DMA((5,)),
    ]
    return pl.pallas_call(
        kernel,
        out_shape=(
            jax.ShapeDtypeStruct((128, 768), BF16),
            jax.ShapeDtypeStruct((3, 256, 256), F32),
        ),
        in_specs=[any_spec, any_spec, any_spec, vmem_spec],
        out_specs=(vmem_spec, vmem_spec),
        scratch_shapes=scratch,
        compiler_params=pltpu.CompilerParams(
            collective_id=0, has_side_effects=True, vmem_limit_bytes=60 * 2**20
        ),
        name="selected_inverse",
    )(ancestor, panels, lists, diag_inverse)


def solution(mesh):
    in_specs = (P("row", "col"), P(None, ("row", "col"), None), P(None, ("row", "col")), P())
    out_specs = (P(("row", "col"), None), P())
    return jax.shard_map(
        per_device, mesh=mesh, in_specs=in_specs, out_specs=out_specs, check_vma=False
    )
```

```python
import jax
import jax.numpy as jnp
from jax import lax
from jax.experimental import pallas as pl
from jax.experimental.pallas import tpu as pltpu
from jax.sharding import PartitionSpec as P

MESH = pl.DeviceIdType.MESH
F32 = jnp.float32
BF16 = jnp.bfloat16
N_SEM = 192
G_ROWS = 16


def mod(value, size):
    return lax.rem(value + 2 * size, size)


def kernel(
    anc_ref, pan_ref, idx_ref, off_ref, diag_ref,
    a_buf, at_buf, g_buf, g_far, i_buf, i_far, part, q1r, q2s, q2r, s_row, s_col, member,
    d_val, d_half, m_val, m_half, d1s, d1r, d2s, d2r, d3s, d3r,
    mcs, mcr, m1s, m1r, m2s, m2r, m3s, m3r, mts, mtr,
    g_send, g_recv, grow, gcol,
    send_sem, recv_sem, load_sem,
):
    row = lax.axis_index("row")
    col = lax.axis_index("col")
    core = lax.rem(row, 2)
    y = lax.rem(lax.div(row, 2), 4)
    x_lo = lax.div(row, 8)
    x_hi = lax.rem(col, 2)
    z = lax.div(col, 2)
    x = x_hi * 2 + x_lo
    where = {"x": x, "y": y, "z": z}

    def device(px, py, pz, pc):
        return (lax.rem(px, 2) * 8 + py * 2 + pc, pz * 2 + lax.div(px, 2))

    def neighbour(axis, step):
        place = dict(where)
        place[axis] = mod(place[axis] + step, 4)
        return device(place["x"], place["y"], place["z"], core)

    partner = (row + 1 - 2 * core, col)
    x_far = (row, col + 1 - 2 * x_hi)
    x_near = (row + 8 - 16 * x_lo, col)
    turn_to = (2 * col + x_lo, y * 2 + core)
    fixed = (turn_to[0] == row) & (turn_to[1] == col)

    used = [0]
    copies = []

    def remote(src, dst, dev):
        n = used[0]
        used[0] += 1
        copy = pltpu.make_async_remote_copy(
            src_ref=src, dst_ref=dst, send_sem=send_sem.at[n], recv_sem=recv_sem.at[n],
            device_id=dev, device_id_type=MESH,
        )
        copies.append(copy)
        return copy

    def send(src, dst, dev):
        copy = remote(src, dst, dev)
        copy.start()
        return copy

    orders = (("x", "y", "z"), ("y", "z", "x"), ("z", "x", "y"))
    loads = []
    for s, (ra, rb, rc) in enumerate(orders):
        loads.append(
            pltpu.make_async_copy(
                pan_ref.at[s], g_buf.at[s, where[rb], where[ra]], load_sem.at[1 + s]
            )
        )
    for one in loads:
        one.start()
    load_a = pltpu.make_async_copy(anc_ref, a_buf, load_sem.at[0])
    load_a.start()

    barrier = pltpu.get_barrier_semaphore()
    for axis in ("x", "y", "z"):
        for step in (1, 3):
            pl.semaphore_signal(
                barrier, inc=1, device_id=neighbour(axis, step), device_id_type=MESH
            )
    pl.semaphore_signal(barrier, inc=1, device_id=partner, device_id_type=MESH)
    lists = idx_ref[...]
    i_buf[z, y, x, pl.ds(0, 3), :] = jnp.concatenate([lists, lists], axis=1)
    for one in loads:
        one.wait()
    pl.semaphore_wait(barrier, 7)

    def gather(axis, whole, half):
        here = where[axis]
        plus, minus = neighbour(axis, 1), neighbour(axis, 3)
        before, after = mod(here + 3, 4), mod(here + 1, 4)
        up = send(whole(here), whole(here), plus)
        down = send(whole(here), whole(here), minus)
        yield
        up.wait_recv()
        up2 = send(half(before, 0), half(before, 0), plus)
        down.wait_recv()
        down2 = send(half(after, 1), half(after, 1), minus)
        yield
        up2.wait_recv()
        down2.wait_recv()
        yield

    def run(*paths):
        for path in paths:
            next(path)

    across = []

    def cross(src, dst):
        across.append(send(src, dst, partner))

    row_start = row * 1024
    col_start = col * 2048

    def mask(i, _):
        r0 = pl.multiple_of(i * 128, 128)
        val = a_buf[pl.ds(r0, 128), :].astype(F32)
        gap = (
            lax.broadcasted_iota(jnp.int32, (128, 2048), 1)
            - lax.broadcasted_iota(jnp.int32, (128, 2048), 0)
            + (col_start - row_start - i * 128)
        )
        a_buf[pl.ds(r0, 128), :] = jnp.where(gap <= 0, val, 0.0).astype(BF16)
        at_buf[:, pl.ds(r0, 128)] = jnp.where(gap < 0, val, 0.0).T.astype(BF16)
        return 0

    ring_a, ring_b = [], []
    for s, (ra, rb, rc) in enumerate(orders):
        g, mb = g_buf.at[s], where[rb]
        ring_a.append(
            gather(ra, lambda i, g=g, mb=mb: g.at[mb, i],
                   lambda i, h, g=g, mb=mb: g.at[mb, i, pl.ds(32 * h, 32)])
        )
        ring_b.append(gather(rb, lambda i, g=g: g.at[i], lambda i, h, g=g: g.at[i, pl.ds(2 * h, 2)]))

    def cross_panels(s, step):
        j = mod(where[orders[s][1]] + step, 4)
        cross(g_buf.at[s, j], g_far.at[s, j])

    ia = gather("x", lambda i: i_buf.at[z, y, i], lambda i, h: i_buf.at[z, y, i, pl.ds(2 * h, 2)])
    ib = gather("y", lambda i: i_buf.at[z, i], lambda i, h: i_buf.at[z, i, pl.ds(2 * h, 2)])
    ic = gather("z", lambda i: i_buf.at[i], lambda i, h: i_buf.at[i, pl.ds(2 * h, 2)])

    run(ia, *ring_a)
    load_a.wait()
    lax.fori_loop(0, 2, mask, 0)
    run(ia, *ring_a)
    lax.fori_loop(2, 3, mask, 0)
    run(ia)
    run(ib)
    for s in range(3):
        run(ring_a[s], ring_b[s])
        cross_panels(s, 0)
    lax.fori_loop(3, 5, mask, 0)
    run(ib)
    for s in range(3):
        run(ring_b[s])
        cross_panels(s, 3)
        cross_panels(s, 1)
    run(ib)
    run(ic)
    lax.fori_loop(5, 7, mask, 0)
    run(ic)
    lax.fori_loop(7, 8, mask, 0)
    run(ic)
    swap_i = send(i_buf, i_far, partner)
    for s in range(3):
        run(ring_b[s])
        cross_panels(s, 2)
    swap_i.wait_recv()

    lane = lax.broadcasted_iota(jnp.int32, (1, 128), 1)
    level = lax.broadcasted_iota(jnp.int32, (128, 128), 0).astype(F32).astype(BF16)

    def spread_part(s):
        ra, rb, rc = orders[s]
        pieces = []
        for buf in (i_buf, i_far):
            for cb in range(4):
                for ca in (0, 2):
                    pos = {rc: where[rc], rb: cb, ra: ca}
                    pos2 = {rc: where[rc], rb: cb, ra: ca + 1}
                    left = buf[pos["z"], pos["y"], pos["x"], pl.ds(s, 1), :]
                    right = buf[pos2["z"], pos2["y"], pos2["x"], pl.ds(s, 1), :]
                    pieces.append(jnp.where(lane < 64, left, right))

        def block(n, _):
            i = lax.div(n, 2)
            t = lax.rem(n, 2)
            place = dict(where)
            place[rc] = i
            to_row, to_col = device(place["x"], place["y"], place["z"], core)
            base = jnp.where(t == 0, to_row * 1024 + to_col * 128, to_col * 2048 + to_row * 128)
            hots = []
            for piece in pieces:
                rel = piece - base
                rel = jnp.where((rel >= 0) & (rel < 128), rel, -1).astype(F32).astype(BF16)
                hots.append(
                    jnp.where(level == rel, jnp.ones((), BF16), jnp.zeros((), BF16))
                )
            near = jnp.concatenate(hots[:8], axis=1)
            far = jnp.concatenate(hots[8:], axis=1)
            out = jnp.dot(near, g_buf[s].reshape(1024, 256), preferred_element_type=F32)
            out = out + jnp.dot(far, g_far[s].reshape(1024, 256), preferred_element_type=F32)
            part[s, i, t] = out.astype(BF16)
            return 0

        lax.fori_loop(0, 8, block, 0)

    def reduce_part(s):
        axis = orders[s][2]
        here = where[axis]
        plus, minus = neighbour(axis, 1), neighbour(axis, 3)
        y1, y2, y3 = mod(here + 1, 4), mod(here + 2, 4), mod(here + 3, 4)
        p1 = send(part.at[s, y2, 0], q1r.at[s, 0], plus)
        n1 = send(part.at[s, y2, 1], q1r.at[s, 1], minus)
        p2b = send(part.at[s, y1, 1], q2r.at[s, 0, 1], plus)
        n2a = send(part.at[s, y3, 0], q2r.at[s, 1, 0], minus)
        yield
        p1.wait_recv()
        q2s[s, 0] = part[s, y1, 0] + q1r[s, 0]
        p2a = send(q2s.at[s, 0], q2r.at[s, 0, 0], plus)
        n1.wait_recv()
        q2s[s, 1] = part[s, y3, 1] + q1r[s, 1]
        n2b = send(q2s.at[s, 1], q2r.at[s, 1, 1], minus)
        yield
        for one in (p2b, n2a, p2a, n2b):
            one.wait_recv()
        cols = pl.ds(s * 256, 256)
        s_row[col, :, cols] = part[s, here, 0] + q2r[s, 0, 0] + q2r[s, 1, 0]
        s_col[row, :, cols] = part[s, here, 1] + q2r[s, 0, 1] + q2r[s, 1, 1]
        yield

    chains = [reduce_part(s) for s in range(3)]
    for s in range(3):
        for n in (s, 3 + 2 * s, 4 + 2 * s, 9 + s):
            across[n].wait_recv()
        spread_part(s)
        run(chains[s])
        if s:
            run(chains[s - 1])
    run(chains[2])
    run(*chains)

    def half_rows(ref):
        return lambda i, h: ref(i).at[pl.ds(64 * h, 64)]

    def row_slot(hi):
        return lambda i: s_row.at[i * 2 + hi]

    def col_slot(lo):
        return lambda i: s_col.at[lo * 8 + i * 2 + core]

    def cross_slot(lo, i):
        ref = col_slot(lo)(i)
        cross(ref, ref)

    def mirrored(i, first):
        c0 = pl.multiple_of(i * 256, 256)
        right = s_row[pl.ds(2 * i, 2)].reshape(256, 768)

        def tile(t, _):
            out = jnp.dot(
                at_buf[pl.ds(t * 256, 256), pl.ds(c0, 256)], right, preferred_element_type=F32
            ).reshape(2, 128, 768)
            m_val[t] = out if first else m_val[t] + out
            return 0

        lax.fori_loop(0, 8, tile, 0)

    def direct(i, first):
        c0 = pl.multiple_of(i * 256, 256)
        c1 = pl.multiple_of(i * 256 + 1024, 256)

        def tile(t, _):
            rows = pl.ds(t * 256, 256)
            out = jnp.dot(
                a_buf[rows, pl.ds(c0, 256)], s_col[pl.ds(2 * i, 2)].reshape(256, 768),
                preferred_element_type=F32,
            ) + jnp.dot(
                a_buf[rows, pl.ds(c1, 256)], s_col[pl.ds(2 * i + 8, 2)].reshape(256, 768),
                preferred_element_type=F32,
            )
            out = out.reshape(2, 128, 768)
            d_val[pl.ds(2 * t, 2)] = out if first else d_val[pl.ds(2 * t, 2)] + out
            return 0

        lax.fori_loop(0, 4, tile, 0)

    y1, y2, y3 = mod(y + 1, 4), mod(y + 2, 4), mod(y + 3, 4)
    z1, z2, z3 = mod(z + 1, 4), mod(z + 2, 4), mod(z + 3, 4)
    across.clear()
    x_row = send(s_row.at[col], s_row.at[col], x_far)
    x_col = send(s_col.at[row], s_col.at[row], x_near)
    z_own = gather("z", row_slot(x_hi), half_rows(row_slot(x_hi)))
    y_own = gather("y", col_slot(x_lo), half_rows(col_slot(x_lo)))
    z_far = gather("z", row_slot(1 - x_hi), half_rows(row_slot(1 - x_hi)))
    y_far = gather("y", col_slot(1 - x_lo), half_rows(col_slot(1 - x_lo)))
    run(y_own, z_own)
    cross_slot(x_lo, y)
    x_col.wait_recv()
    run(y_far)
    cross_slot(1 - x_lo, y)
    x_row.wait_recv()
    run(z_far)
    run(y_own, z_own)
    cross_slot(x_lo, y3)
    cross_slot(x_lo, y1)
    mirrored(z, True)
    across[0].wait_recv()
    across[1].wait_recv()
    direct(y, True)
    run(y_far, z_far)
    cross_slot(1 - x_lo, y3)
    cross_slot(1 - x_lo, y1)
    mirrored(z3, False)
    mirrored(z1, False)
    for one in across[2:6]:
        one.wait_recv()
    direct(y3, False)
    run(y_own)
    cross_slot(x_lo, y2)
    run(y_far)
    cross_slot(1 - x_lo, y2)
    direct(y1, False)
    run(z_own)
    run(z_far)

    right = s_row[pl.ds(2 * z2, 2)].reshape(256, 768)
    c0 = pl.multiple_of(z2 * 256, 256)
    m_across = {}
    for name, place in (("2", y2), ("1", y1), ("3", y3), ("0", y)):
        for lo in (0, 1):
            t = lo * 4 + place
            rows = pl.ds(pl.multiple_of(t * 256, 256), 256)
            out = jnp.dot(at_buf[rows, pl.ds(c0, 256)], right, preferred_element_type=F32)
            out = m_val[t] + out.reshape(2, 128, 768)
            m_val[t] = out
            m_half[rows, :] = out.reshape(256, 768).astype(BF16)
            mcs[t] = m_half[pl.ds(pl.multiple_of(t * 256 + (1 - core) * 128, 128), 128), :]
            m_across[name, lo] = send(mcs.at[t], mcr.at[t], partner)

    for one in across[6:]:
        one.wait_recv()
    e0 = pl.multiple_of(y2 * 256, 256)
    e1 = pl.multiple_of(y2 * 256 + 1024, 256)

    def direct_last(t):
        rows = pl.ds(pl.multiple_of(t * 256, 256), 256)
        out = jnp.dot(
            a_buf[rows, pl.ds(e0, 256)], s_col[pl.ds(2 * y2, 2)].reshape(256, 768),
            preferred_element_type=F32,
        ) + jnp.dot(
            a_buf[rows, pl.ds(e1, 256)], s_col[pl.ds(2 * y2 + 8, 2)].reshape(256, 768),
            preferred_element_type=F32,
        )
        out = d_val[pl.ds(2 * t, 2)] + out.reshape(2, 128, 768)
        d_val[pl.ds(2 * t, 2)] = out
        d_half[rows, :] = out.reshape(256, 768).astype(BF16)

    def reduce_column():
        def val(lo, i):
            n = lo * 4 + i
            return m_val[n, core] + mcr[n].astype(F32)

        plus, minus = neighbour("y", 1), neighbour("y", 3)
        m_across["2", 0].wait_recv()
        m1s[0] = val(0, y2).astype(BF16)
        p1 = send(m1s.at[0], m1r.at[0], plus)
        m_across["2", 1].wait_recv()
        m1s[1] = val(1, y2).astype(BF16)
        n1 = send(m1s.at[1], m1r.at[1], minus)
        m_across["1", 1].wait_recv()
        m2s[0, 1] = val(1, y1).astype(BF16)
        p2b = send(m2s.at[0, 1], m2r.at[0, 1], plus)
        m_across["3", 0].wait_recv()
        m2s[1, 0] = val(0, y3).astype(BF16)
        n2a = send(m2s.at[1, 0], m2r.at[1, 0], minus)
        yield
        p1.wait_recv()
        m_across["1", 0].wait_recv()
        m2s[0, 0] = (val(0, y1) + m1r[0].astype(F32)).astype(BF16)
        p2a = send(m2s.at[0, 0], m2r.at[0, 0], plus)
        n1.wait_recv()
        m_across["3", 1].wait_recv()
        m2s[1, 1] = (val(1, y3) + m1r[1].astype(F32)).astype(BF16)
        n2b = send(m2s.at[1, 1], m2r.at[1, 1], minus)
        yield
        m_across["0", 0].wait_recv()
        m_across["0", 1].wait_recv()
        for one in (p2b, n2a, p2a, n2b):
            one.wait_recv()

        def total(lo):
            return val(lo, y) + m2r[0, lo].astype(F32) + m2r[1, lo].astype(F32)

        m3s[...] = total(1 - x_lo).astype(BF16)
        e = send(m3s, m3r, x_near)
        yield
        e.wait_recv()
        yield total(x_lo) + m3r[...].astype(F32)

    def reduce_row():
        plus, minus = neighbour("z", 1), neighbour("z", 3)
        direct_last(z2)
        d1s[0] = d_val[z2 * 2].astype(BF16)
        p1 = send(d1s.at[0], d1r.at[0], plus)
        d1s[1] = d_val[z2 * 2 + 1].astype(BF16)
        n1 = send(d1s.at[1], d1r.at[1], minus)
        direct_last(z1)
        d2s[0, 1] = d_val[z1 * 2 + 1].astype(BF16)
        p2b = send(d2s.at[0, 1], d2r.at[0, 1], plus)
        direct_last(z3)
        d2s[1, 0] = d_val[z3 * 2].astype(BF16)
        n2a = send(d2s.at[1, 0], d2r.at[1, 0], minus)
        yield
        p1.wait_recv()
        d2s[0, 0] = (d_val[z1 * 2] + d1r[0].astype(F32)).astype(BF16)
        p2a = send(d2s.at[0, 0], d2r.at[0, 0], plus)
        n1.wait_recv()
        d2s[1, 1] = (d_val[z3 * 2 + 1] + d1r[1].astype(F32)).astype(BF16)
        n2b = send(d2s.at[1, 1], d2r.at[1, 1], minus)
        yield
        for one in (p2b, n2a, p2a, n2b):
            one.wait_recv()

        def total(hi):
            return d_val[z * 2 + hi] + d2r[0, hi].astype(F32) + d2r[1, hi].astype(F32)

        d3s[...] = total(1 - x_hi).astype(BF16)
        e = send(d3s, d3r, x_far)
        yield
        e.wait_recv()
        yield total(x_hi) + d3r[...].astype(F32)

    d_path = reduce_row()
    m_path = reduce_column()
    run(d_path)
    run(m_path)
    direct_last(z)

    along = (((0,), (0,)), ((), ()))
    for s in range(3):
        cols = pl.ds(s * 256, 256)
        out = lax.dot_general(
            s_row[:, :, cols].reshape(1024, 256), d_half[:, cols], along, preferred_element_type=F32
        ) + lax.dot_general(
            s_col[:, :, cols].reshape(2048, 256), m_half[:, cols], along, preferred_element_type=F32
        )
        g_send[:, :, cols] = out.astype(BF16).reshape(16, G_ROWS, 256)

    column = [mod(row + step, 16) for step in range(1, 16)]
    sends = [send(g_send.at[r], g_recv.at[row], (r, col)) for r in column]
    run(d_path)
    run(m_path)

    own_rows = lax.broadcasted_iota(jnp.int32, (128, 128), 0) + (row * 1024 + col * 128)
    for s in range(3):
        def seen(n, found, s=s):
            pz, py = lax.div(n, 4), lax.rem(n, 4)
            for buf in (i_buf, i_far):
                for px in (0, 2):
                    left = buf[pz, py, px, pl.ds(s, 1), :]
                    right = buf[pz, py, px + 1, pl.ds(s, 1), :]
                    line = jnp.where(lane < 64, left, right)
                    found = jnp.where(own_rows == line, 1.0, found)
            return found
        found = lax.fori_loop(0, 16, seen, jnp.zeros((128, 128), F32))
        flag = jnp.max(found, axis=1, keepdims=True)
        member[:, pl.ds(s * 256, 256)] = jnp.broadcast_to(flag, (128, 256))

    for one in sends:
        one.wait_recv()
    total = g_send[row].astype(F32)
    for r in column:
        total = total + g_recv[r].astype(F32)
    grow[col] = total.astype(BF16)
    sends = [
        send(grow.at[col], grow.at[col], (row, mod(col + step, 8))) for step in range(1, 8)
    ]
    run(d_path)
    run(m_path)
    for one in sends:
        one.wait_recv()
    total = grow[0].astype(F32)
    for n in range(1, 8):
        total = total + grow[n].astype(F32)
    gcol[row] = total.astype(BF16)
    sends = [send(gcol.at[row], gcol.at[row], (r, col)) for r in column]

    mts[...] = next(m_path).astype(BF16)
    turn = remote(mts, mtr, turn_to)

    @pl.when(jnp.logical_not(fixed))
    def _():
        turn.start()

    @pl.when(fixed)
    def _():
        mtr[...] = mts[...]

    d_own = next(d_path)
    for one in sends:
        one.wait_recv()
    for s in range(3):
        diag_ref[s] = gcol[:, :, pl.ds(s * 256, 256)].astype(F32).reshape(256, 256)

    @pl.when(jnp.logical_not(fixed))
    def _():
        turn.wait_recv()

    product = d_own + mtr[...].astype(F32)
    off_ref[...] = jnp.where(member[...] > 0.5, product, 0.0).astype(BF16)

    for one in copies:
        if one is not turn:
            one.wait_send()

    @pl.when(jnp.logical_not(fixed))
    def _():
        turn.wait_send()


def per_device(ancestor, panels, row_index, diag_inverse):
    V = pltpu.VMEM
    any_spec = pl.BlockSpec(memory_space=pl.ANY)
    vmem_spec = pl.BlockSpec(memory_space=pltpu.VMEM)
    slice_shape = (128, 768)

    scratch = [
        V((1024, 2048), BF16), V((2048, 1024), BF16),
        V((3, 4, 4, 64, 256), BF16), V((3, 4, 4, 64, 256), BF16),
        V((4, 4, 4, 4, 128), jnp.int32), V((4, 4, 4, 4, 128), jnp.int32),
        V((3, 4, 2, 128, 256), BF16), V((3, 2, 128, 256), BF16),
        V((3, 2, 128, 256), BF16), V((3, 2, 2, 128, 256), BF16),
        V((8, *slice_shape), BF16), V((16, *slice_shape), BF16), V(slice_shape, F32),
        V((8, *slice_shape), F32), V((1024, 768), BF16),
        V((8, 2, *slice_shape), F32), V((2048, 768), BF16),
        V((2, *slice_shape), BF16), V((2, *slice_shape), BF16),
        V((2, 2, *slice_shape), BF16), V((2, 2, *slice_shape), BF16),
        V(slice_shape, BF16), V(slice_shape, BF16),
        V((8, *slice_shape), BF16), V((8, *slice_shape), BF16),
        V((2, *slice_shape), BF16), V((2, *slice_shape), BF16),
        V((2, 2, *slice_shape), BF16), V((2, 2, *slice_shape), BF16),
        V(slice_shape, BF16), V(slice_shape, BF16), V(slice_shape, BF16), V(slice_shape, BF16),
        V((16, G_ROWS, 768), BF16), V((16, G_ROWS, 768), BF16),
        V((8, G_ROWS, 768), BF16), V((16, G_ROWS, 768), BF16),
        pltpu.SemaphoreType.DMA((N_SEM,)), pltpu.SemaphoreType.DMA((N_SEM,)),
        pltpu.SemaphoreType.DMA((4,)),
    ]
    kept, blocks = pl.pallas_call(
        kernel,
        out_shape=(
            jax.ShapeDtypeStruct((128, 768), BF16),
            jax.ShapeDtypeStruct((3, 256, 256), F32),
        ),
        in_specs=[any_spec, any_spec, vmem_spec],
        out_specs=(vmem_spec, vmem_spec),
        scratch_shapes=scratch,
        compiler_params=pltpu.CompilerParams(
            collective_id=0, has_side_effects=True, vmem_limit_bytes=60 * 2**20
        ),
        name="selected_inverse",
    )(ancestor, panels, row_index)
    return 0 - kept, diag_inverse + blocks


def solution(mesh):
    in_specs = (P("row", "col"), P(None, ("row", "col"), None), P(None, ("row", "col")), P())
    out_specs = (P(("row", "col"), None), P())
    return jax.shard_map(
        per_device, mesh=mesh, in_specs=in_specs, out_specs=out_specs, check_vma=False
    )
```

```python
import jax
import jax.numpy as jnp
from jax import lax
from jax.experimental import pallas as pl
from jax.experimental.pallas import tpu as pltpu
from jax.sharding import PartitionSpec as P

MESH = pl.DeviceIdType.MESH
F32 = jnp.float32
BF16 = jnp.bfloat16
N_SEM = 288
G_ROWS = 16


def mod(value, size):
    return lax.rem(value + 2 * size, size)


ORDER = (
    "0P 1P 2P 0R2", "1R2 2R2 0R3 1R3", "2R3 0Y1 0Z1 1Y1", "1Z1 2Y1 2Z1 0Y2", "1Y2 2Y2 0Z2 0Y3",
    "0Z3 0Y4 1Z2 0Z4", "0Y5 0Z5 0M 1Y3", "1Z3 1Y4 1Z4 2Z2", "0D 1Y5 1Z5 2Y3", "2Z3 0M1 1M 2Y4",
    "2Z4 1D 0D2 0M2", "2Y5 1M1 2Z5 2M", "0G 0D3 0M3 2D", "1G 2M1 1D2 1M2", "2G g0 0M4 f0",
    "f1 f2 2D2 2M2", "g1 1D3 1M3 g2", "0F 2D3 2M3 1M4", "g3 1F 2M4 g4", "2F g5",
)


def kernel(
    anc_ref, pan_ref, idx_ref, off_ref, diag_ref,
    a_buf, at_buf, g_buf, i_own, i_buf, i_far, i_mix, part, q1r, q2s, q2r, s_row, s_col, member,
    d_half, m_half, d2s, d1r, d2r, d3s, d3r,
    mcr, m1s, m1r, m2s, m2r, m3s, m3r, mts, mtr,
    g_send, g_swap, g_half, g_recv, grow, gcol,
    send_sem, recv_sem, load_sem,
):
    row = lax.axis_index("row")
    col = lax.axis_index("col")
    core = lax.rem(row, 2)
    y = lax.rem(lax.div(row, 2), 4)
    x_lo = lax.div(row, 8)
    x_hi = lax.rem(col, 2)
    z = lax.div(col, 2)
    x = x_hi * 2 + x_lo
    where = {"x": x, "y": y, "z": z}
    y1, y2, y3 = mod(y + 1, 4), mod(y + 2, 4), mod(y + 3, 4)
    z1, z2, z3 = mod(z + 1, 4), mod(z + 2, 4), mod(z + 3, 4)

    def device(px, py, pz, pc):
        return (lax.rem(px, 2) * 8 + py * 2 + pc, pz * 2 + lax.div(px, 2))

    def neighbour(axis, step):
        place = dict(where)
        place[axis] = mod(place[axis] + step, 4)
        return device(place["x"], place["y"], place["z"], core)

    partner = (row + 1 - 2 * core, col)
    x_far = (row, col + 1 - 2 * x_hi)
    x_near = (row + 8 - 16 * x_lo, col)
    turned = lax.rem(col, 4)
    turn_to = (2 * col + x_lo, lax.rem(y + turned, 4) * 2 + core)
    fixed = (turn_to[0] == row) & (turn_to[1] == col)
    lane = lax.broadcasted_iota(jnp.int32, (1, 128), 1)

    used = [0]
    copies = []

    def remote(src, dst, dev):
        n = used[0]
        used[0] += 1
        copy = pltpu.make_async_remote_copy(
            src_ref=src, dst_ref=dst, send_sem=send_sem.at[n], recv_sem=recv_sem.at[n],
            device_id=dev, device_id_type=MESH,
        )
        copies.append(copy)
        return copy

    def send(src, dst, dev):
        copy = remote(src, dst, dev)
        copy.start()
        return copy

    orders = (("x", "y", "z"), ("y", "z", "x"), ("z", "x", "y"))
    loads = []
    for s, (ra, rb, rc) in enumerate(orders):
        loads.append(
            pltpu.make_async_copy(
                pan_ref.at[s], g_buf.at[s, where[rb], where[ra], core], load_sem.at[1 + s]
            )
        )
    load_i = pltpu.make_async_copy(idx_ref, i_own, load_sem.at[4])
    load_i.start()
    for one in loads:
        one.start()
    load_a = pltpu.make_async_copy(anc_ref, a_buf, load_sem.at[0])
    load_a.start()

    barrier = pltpu.get_barrier_semaphore()
    for axis in ("x", "y", "z"):
        for step in (1, 2, 3):
            pl.semaphore_signal(
                barrier, inc=1, device_id=neighbour(axis, step), device_id_type=MESH
            )
    pl.semaphore_signal(barrier, inc=1, device_id=partner, device_id_type=MESH)
    load_i.wait()
    lists = i_own[...]
    twice = jnp.concatenate([lists, lists], axis=1)
    for s, (ra, rb, rc) in enumerate(orders):
        i_buf[s, where[rb], where[ra], pl.ds(0, 3), :] = twice
        i_buf[s, where[rb], where[ra], pl.ds(3, 1), :] = twice[:1]
    for one in loads:
        one.wait()
    pl.semaphore_wait(barrier, 10)

    def gather(axis, whole, half):
        here = where[axis]
        plus, minus = neighbour(axis, 1), neighbour(axis, 3)
        before, after = mod(here + 3, 4), mod(here + 1, 4)
        up = send(whole(here), whole(here), plus)
        down = send(whole(here), whole(here), minus)
        yield
        up.wait_recv()
        up2 = send(half(before, 0), half(before, 0), plus)
        down.wait_recv()
        down2 = send(half(after, 1), half(after, 1), minus)
        yield
        up2.wait_recv()
        down2.wait_recv()
        yield

    def gather_short(axis, whole):
        here = where[axis]
        sent = [send(whole(here), whole(here), neighbour(axis, step)) for step in (1, 3, 2)]
        yield
        for one in sent:
            one.wait_recv()
        yield

    def run(*paths):
        for path in paths:
            next(path)

    across = {}

    def cross(key, ref):
        across[key] = send(ref, ref, partner)

    row_start = row * 1024
    col_start = col * 2048

    def mask(i, _):
        r0 = pl.multiple_of(i * 128, 128)
        val = a_buf[pl.ds(r0, 128), :].astype(F32)
        gap = (
            lax.broadcasted_iota(jnp.int32, (128, 2048), 1)
            - lax.broadcasted_iota(jnp.int32, (128, 2048), 0)
            + (col_start - row_start - i * 128)
        )
        a_buf[pl.ds(r0, 128), :] = jnp.where(gap <= 0, val, 0.0).astype(BF16)
        at_buf[:, pl.ds(r0, 128)] = jnp.where(gap < 0, val, 0.0).T.astype(BF16)
        return 0

    ring_a, ring_b, list_a, list_b, list_c = [], [], [], [], []
    for s, (ra, rb, rc) in enumerate(orders):
        g, own, mix, mb = g_buf.at[s], i_buf.at[s], i_mix.at[s], where[rb]
        ring_a.append(gather_short(ra, lambda i, g=g, mb=mb: g.at[mb, i, core]))
        ring_b.append(
            gather(rb, lambda i, g=g: g.at[i, :, core],
                   lambda i, h, g=g: g.at[i, pl.ds(2 * h, 2), core])
        )
        list_a.append(gather_short(ra, lambda i, own=own, mb=mb: own.at[mb, i]))
        list_b.append(gather_short(rb, lambda i, own=own: own.at[i]))
        list_c.append(gather_short(rc, lambda i, mix=mix: mix.at[i]))

    def cross_panels(s, step):
        j = mod(where[orders[s][1]] + step, 4)
        cross((s, "g", step), g_buf.at[s, j, :, core])

    run(*ring_a, *list_a)
    load_a.wait()
    lax.fori_loop(0, 4, mask, 0)
    for s in range(3):
        run(ring_a[s], ring_b[s])
    for s in range(3):
        run(list_a[s], list_b[s])
        cross_panels(s, 0)
    lax.fori_loop(4, 6, mask, 0)
    for s in range(3):
        run(ring_b[s])
    for s in range(3):
        cross_panels(s, 3)
        cross_panels(s, 1)
        run(list_b[s])
        across[s, "i"] = send(i_buf.at[s], i_far.at[s], partner)
    lax.fori_loop(6, 8, mask, 0)
    for s in range(3):
        run(ring_b[s])
        cross_panels(s, 2)
    for s in range(3):
        across[s, "i"].wait_recv()
        i_mix[s, where[orders[s][2]]] = jnp.where(
            (lane < 64) == (core == 0), i_buf[s], i_far[s]
        )
        run(list_c[s])

    level = lax.broadcasted_iota(jnp.int32, (128, 128), 0).astype(F32).astype(BF16)

    def spread_part(s):
        rc = orders[s][2]
        pieces = [
            i_mix[s, where[rc], cb, ca, pl.ds(s, 1), :] for cb in range(4) for ca in range(4)
        ]

        def block(i, _):
            place = dict(where)
            place[rc] = i
            to_row, to_col = device(place["x"], place["y"], place["z"], core)
            halves = []
            for base in (to_row * 1024 + to_col * 128, to_col * 2048 + to_row * 128):
                hots = []
                for piece in pieces:
                    rel = piece - base
                    rel = jnp.where((rel >= 0) & (rel < 128), rel, -1).astype(F32).astype(BF16)
                    hots.append(jnp.where(level == rel, jnp.ones((), BF16), jnp.zeros((), BF16)))
                halves.append(jnp.concatenate(hots, axis=1))
            out = jnp.dot(
                jnp.concatenate(halves, axis=0), g_buf[s].reshape(2048, 256),
                preferred_element_type=F32,
            )
            part[s, i] = out.astype(BF16).reshape(2, 128, 256)
            return 0

        lax.fori_loop(0, 4, block, 0)

    def mirrored(s):
        def tile(t, _):
            rows = pl.ds(pl.multiple_of(t * 1024, 1024), 1024)
            out = jnp.dot(
                at_buf[rows, :], s_row[s].reshape(1024, 256), preferred_element_type=F32
            )
            m_half[s, pl.ds(4 * t, 4)] = out.astype(BF16).reshape(4, 2, 128, 256)
            return 0

        lax.fori_loop(0, 2, tile, 0)

    def direct(s):
        def tile(t, _):
            rows = pl.ds(pl.multiple_of(t * 512, 512), 512)
            out = jnp.dot(
                a_buf[rows, :], s_col[s].reshape(2048, 256), preferred_element_type=F32
            )
            d_half[s, pl.ds(4 * t, 4)] = out.astype(BF16).reshape(4, 128, 256)
            return 0

        lax.fori_loop(0, 2, tile, 0)

    along = (((0,), (0,)), ((), ()))
    x_plus, x_minus = neighbour("x", 1), neighbour("x", 3)
    y_plus, y_minus = neighbour("y", 1), neighbour("y", 3)
    z_plus, z_minus = neighbour("z", 1), neighbour("z", 3)

    steps = {}

    def flow(names, path):
        for name in names:
            steps[name] = path

    turns = []

    def spread(s):
        axis = orders[s][2]
        here = where[axis]
        plus, minus = neighbour(axis, 1), neighbour(axis, 3)
        h1, h2, h3 = mod(here + 1, 4), mod(here + 2, 4), mod(here + 3, 4)
        for step in range(4):
            across[s, "g", step].wait_recv()
        spread_part(s)
        p1 = send(part.at[s, h2, 0], q1r.at[s, 0], plus)
        n1 = send(part.at[s, h2, 1], q1r.at[s, 1], minus)
        p2b = send(part.at[s, h1, 1], q2r.at[s, 0, 1], plus)
        n2a = send(part.at[s, h3, 0], q2r.at[s, 1, 0], minus)
        yield
        p1.wait_recv()
        q2s[s, 0] = part[s, h1, 0] + q1r[s, 0]
        p2a = send(q2s.at[s, 0], q2r.at[s, 0, 0], plus)
        n1.wait_recv()
        q2s[s, 1] = part[s, h3, 1] + q1r[s, 1]
        n2b = send(q2s.at[s, 1], q2r.at[s, 1, 1], minus)
        yield
        for one in (p2b, n2a, p2a, n2b):
            one.wait_recv()
        s_row[s, col] = part[s, here, 0] + q2r[s, 0, 0] + q2r[s, 1, 0]
        s_col[s, row] = part[s, here, 1] + q2r[s, 0, 1] + q2r[s, 1, 1]
        flow([f"{s}Y{n}" for n in range(1, 6)], column_rows(s))
        flow([f"{s}Z{n}" for n in range(1, 6)], row_rows(s))
        run(steps[f"{s}Y1"], steps[f"{s}Z1"])
        yield

    def half_rows(ref):
        return lambda i, h: ref(i).at[pl.ds(64 * h, 64)]

    def column_rows(s):
        def slot(lo):
            return lambda i: s_col.at[s, lo * 8 + i * 2 + core]

        def cross_slot(name, lo, i):
            cross((s, name), slot(lo)(i))

        own = gather("y", slot(x_lo), half_rows(slot(x_lo)))
        far = gather("y", slot(1 - x_lo), half_rows(slot(1 - x_lo)))
        near = send(s_col.at[s, row], s_col.at[s, row], x_near)
        run(own)
        cross_slot("o0", x_lo, y)
        yield
        run(own)
        cross_slot("o3", x_lo, y3)
        cross_slot("o1", x_lo, y1)
        yield
        near.wait_recv()
        run(far)
        cross_slot("f0", 1 - x_lo, y)
        yield
        run(own)
        cross_slot("o2", x_lo, y2)
        yield
        run(far)
        cross_slot("f3", 1 - x_lo, y3)
        cross_slot("f1", 1 - x_lo, y1)
        yield
        run(far)
        cross_slot("f2", 1 - x_lo, y2)
        yield

    def row_rows(s):
        def slot(hi):
            return lambda i: s_row.at[s, i * 2 + hi]

        own = gather("z", slot(x_hi), half_rows(slot(x_hi)))
        far = gather("z", slot(1 - x_hi), half_rows(slot(1 - x_hi)))
        away = send(s_row.at[s, col], s_row.at[s, col], x_far)
        run(own)
        yield
        run(own)
        yield
        away.wait_recv()
        run(far)
        yield
        run(own)
        yield
        run(far)
        yield
        run(far)
        yield

    def mirrored_sum(s):
        mirrored(s)
        m0 = send(m_half.at[s, :, 1 - core], mcr.at[s], partner)
        yield
        m0.wait_recv()

        def val(lo, i):
            n = lo * 4 + mod(i + turned, 4)
            return m_half[s, n, core].astype(F32) + mcr[s, n].astype(F32)

        m1s[s, 0] = val(0, y2).astype(BF16)
        p1 = send(m1s.at[s, 0], m1r.at[s, 0], y_plus)
        m1s[s, 1] = val(1, y2).astype(BF16)
        n1 = send(m1s.at[s, 1], m1r.at[s, 1], y_minus)
        m2s[s, 0, 1] = val(1, y1).astype(BF16)
        p2b = send(m2s.at[s, 0, 1], m2r.at[s, 0, 1], y_plus)
        m2s[s, 1, 0] = val(0, y3).astype(BF16)
        n2a = send(m2s.at[s, 1, 0], m2r.at[s, 1, 0], y_minus)
        yield
        p1.wait_recv()
        m2s[s, 0, 0] = (val(0, y1) + m1r[s, 0].astype(F32)).astype(BF16)
        p2a = send(m2s.at[s, 0, 0], m2r.at[s, 0, 0], y_plus)
        n1.wait_recv()
        m2s[s, 1, 1] = (val(1, y3) + m1r[s, 1].astype(F32)).astype(BF16)
        n2b = send(m2s.at[s, 1, 1], m2r.at[s, 1, 1], y_minus)
        yield
        for one in (p2b, n2a, p2a, n2b):
            one.wait_recv()
        def total(lo):
            return val(lo, y) + m2r[s, 0, lo].astype(F32) + m2r[s, 1, lo].astype(F32)

        m3s[s] = total(1 - x_lo).astype(BF16)
        e = send(m3s.at[s], m3r.at[s], x_near)
        yield
        e.wait_recv()
        mts[s] = (total(x_lo) + m3r[s].astype(F32)).astype(BF16)
        turn = remote(mts.at[s], mtr.at[s], turn_to)

        @pl.when(jnp.logical_not(fixed))
        def _():
            turn.start()

        @pl.when(fixed)
        def _():
            mtr[s] = mts[s]

        turns.append(turn)
        yield

        @pl.when(jnp.logical_not(fixed))
        def _():
            turn.wait_recv()

        yield mtr[s].astype(F32)

    def direct_sum(s):
        for name in ("o0", "o3", "o1", "f0", "o2", "f3", "f1", "f2"):
            across[s, name].wait_recv()
        direct(s)
        p1 = send(d_half.at[s, z2 * 2], d1r.at[s, 0], z_plus)
        n1 = send(d_half.at[s, z2 * 2 + 1], d1r.at[s, 1], z_minus)
        p2b = send(d_half.at[s, z1 * 2 + 1], d2r.at[s, 0, 1], z_plus)
        n2a = send(d_half.at[s, z3 * 2], d2r.at[s, 1, 0], z_minus)
        yield
        p1.wait_recv()
        d2s[s, 0] = (d_half[s, z1 * 2].astype(F32) + d1r[s, 0].astype(F32)).astype(BF16)
        p2a = send(d2s.at[s, 0], d2r.at[s, 0, 0], z_plus)
        n1.wait_recv()
        d2s[s, 1] = (d_half[s, z3 * 2 + 1].astype(F32) + d1r[s, 1].astype(F32)).astype(BF16)
        n2b = send(d2s.at[s, 1], d2r.at[s, 1, 1], z_minus)
        yield
        for one in (p2b, n2a, p2a, n2b):
            one.wait_recv()

        def total(hi):
            return (
                d_half[s, z * 2 + hi].astype(F32)
                + d2r[s, 0, hi].astype(F32) + d2r[s, 1, hi].astype(F32)
            )

        d3s[s] = total(1 - x_hi).astype(BF16)
        e = send(d3s.at[s], d3r.at[s], x_far)
        yield
        e.wait_recv()
        yield total(x_hi) + d3r[s].astype(F32)

    def finish(s):
        product = next(steps[f"{s}M"]) + next(steps[f"{s}D"])
        off_ref[:, pl.ds(s * 256, 256)] = jnp.where(member[s] > 0.5, product, 0.0).astype(BF16)
        yield

    def share(s):
        out = lax.dot_general(
            s_row[s].reshape(1024, 256), d_half[s].reshape(1024, 256), along,
            preferred_element_type=F32,
        ) + lax.dot_general(
            s_col[s].reshape(2048, 256), m_half[s].reshape(2048, 256), along,
            preferred_element_type=F32,
        )
        g_send[:, :, :, pl.ds(s * 256, 256)] = out.astype(BF16).reshape(8, 2, G_ROWS, 256)
        yield


    near = [(lax.rem(lax.div(row, 2) + n, 8)) for n in range(1, 8)]
    pair = lax.div(row, 2)

    def diagonal():
        swap = send(g_send.at[:, 1 - core], g_swap, partner)
        yield
        swap.wait_recv()
        for n in range(8):
            g_half[n] = (g_send[n, core].astype(F32) + g_swap[n].astype(F32)).astype(BF16)
        sends = [send(g_half.at[n], g_recv.at[pair], (2 * n + core, col)) for n in near]
        yield
        for one in sends:
            one.wait_recv()
        total = g_half[pair].astype(F32)
        for n in near:
            total = total + g_recv[n].astype(F32)
        grow[col] = total.astype(BF16)
        sends = [
            send(grow.at[col], grow.at[col], (row, mod(col + step, 8))) for step in range(1, 8)
        ]
        yield
        for one in sends:
            one.wait_recv()
        total = grow[0].astype(F32)
        for n in range(1, 8):
            total = total + grow[n].astype(F32)
        mine = gcol.at[pair, core]
        gcol[pair, core] = total.astype(BF16)
        sends = [send(mine, mine, (2 * n + core, col)) for n in near]
        across_own = send(mine, mine, partner)
        yield
        for one in sends:
            one.wait_recv()
        across_all = [send(gcol.at[n, core], gcol.at[n, core], partner) for n in near]
        yield
        across_own.wait_recv()
        for one in across_all:
            one.wait_recv()
        for s in range(3):
            diag_ref[s] = gcol[:, :, :, pl.ds(s * 256, 256)].astype(F32).reshape(256, 256)
        yield

    def flags(s):
        run(list_c[s])
        own_rows = lax.broadcasted_iota(jnp.int32, (128, 128), 0) + (row * 1024 + col * 128)

        def seen(n, found):
            pz, py = lax.div(n, 4), lax.rem(n, 4)
            for px in range(4):
                line = i_mix[s, pz, py, px, pl.ds(s, 1), :]
                found = jnp.where(own_rows == line, 1.0, found)
            return found

        found = lax.fori_loop(0, 16, seen, jnp.zeros((128, 128), F32))
        flag = jnp.max(found, axis=1, keepdims=True)
        member[s] = jnp.broadcast_to(flag, (128, 256))
        yield

    for s in range(3):
        flow([f"{s}P", f"{s}R2", f"{s}R3"], spread(s))
        flow([f"{s}M"] + [f"{s}M{n}" for n in range(1, 5)], mirrored_sum(s))
        flow([f"{s}D", f"{s}D2", f"{s}D3"], direct_sum(s))
        flow([f"{s}G"], share(s))
        flow([f"{s}F"], finish(s))
        flow([f"f{s}"], flags(s))
    flow([f"g{n}" for n in range(6)], diagonal())
    for name in " ".join(ORDER).split():
        run(steps[name])

    for one in copies:
        if all(one is not turn for turn in turns):
            one.wait_send()

    @pl.when(jnp.logical_not(fixed))
    def _():
        for turn in turns:
            turn.wait_send()


def per_device(ancestor, panels, row_index, diag_inverse):
    V = pltpu.VMEM
    any_spec = pl.BlockSpec(memory_space=pltpu.HBM)
    vmem_spec = pl.BlockSpec(memory_space=pltpu.VMEM)
    piece = (128, 256)

    scratch = [
        V((1024, 2048), BF16), V((2048, 1024), BF16),
        V((3, 4, 4, 2, 64, 256), BF16),
        V((3, 64), jnp.int32), V((3, 4, 4, 4, 128), jnp.int32), V((3, 4, 4, 4, 128), jnp.int32),
        V((3, 4, 4, 4, 4, 128), jnp.int32),
        V((3, 4, 2, *piece), BF16), V((3, 2, *piece), BF16),
        V((3, 2, *piece), BF16), V((3, 2, 2, *piece), BF16),
        V((3, 8, *piece), BF16), V((3, 16, *piece), BF16), V((3, *piece), F32),
        V((3, 8, *piece), BF16), V((3, 8, 2, *piece), BF16),
        V((3, 2, *piece), BF16), V((3, 2, *piece), BF16), V((3, 2, 2, *piece), BF16),
        V((3, *piece), BF16), V((3, *piece), BF16),
        V((3, 8, *piece), BF16),
        V((3, 2, *piece), BF16), V((3, 2, *piece), BF16),
        V((3, 2, 2, *piece), BF16), V((3, 2, 2, *piece), BF16),
        V((3, *piece), BF16), V((3, *piece), BF16), V((3, *piece), BF16), V((3, *piece), BF16),
        V((8, 2, G_ROWS, 768), BF16), V((8, G_ROWS, 768), BF16), V((8, G_ROWS, 768), BF16),
        V((8, G_ROWS, 768), BF16), V((8, G_ROWS, 768), BF16), V((8, 2, G_ROWS, 768), BF16),
        pltpu.SemaphoreType.DMA((N_SEM,)), pltpu.SemaphoreType.DMA((N_SEM,)),
        pltpu.SemaphoreType.DMA((5,)),
    ]
    ancestor = pltpu.with_memory_space_constraint(ancestor, pltpu.HBM)
    panels = pltpu.with_memory_space_constraint(panels, pltpu.HBM)
    row_index = pltpu.with_memory_space_constraint(row_index, pltpu.HBM)
    kept, blocks = pl.pallas_call(
        kernel,
        out_shape=(
            jax.ShapeDtypeStruct((128, 768), BF16),
            jax.ShapeDtypeStruct((3, 256, 256), F32),
        ),
        in_specs=[any_spec, any_spec, any_spec],
        out_specs=(vmem_spec, vmem_spec),
        scratch_shapes=scratch,
        compiler_params=pltpu.CompilerParams(
            collective_id=0, has_side_effects=True, vmem_limit_bytes=48 * 2**20
        ),
        name="selected_inverse",
    )(ancestor, panels, row_index)
    return 0 - kept, diag_inverse + blocks


def solution(mesh):
    in_specs = (P("row", "col"), P(None, ("row", "col"), None), P(None, ("row", "col")), P())
    out_specs = (P(("row", "col"), None), P())
    return jax.shard_map(
        per_device, mesh=mesh, in_specs=in_specs, out_specs=out_specs, check_vma=False
    )
```

```python
import jax
import jax.numpy as jnp
from jax import lax
from jax.experimental import pallas as pl
from jax.experimental.pallas import tpu as pltpu
from jax.sharding import PartitionSpec as P

MESH = pl.DeviceIdType.MESH
F32 = jnp.float32
BF16 = jnp.bfloat16
N_SEM = 336
G_ROWS = 16


def mod(value, size):
    return lax.rem(value + 2 * size, size)


ORDER = (
    "0P 1P 0R2 2P", "1R2 0R3 2R2 0Y1", "0Z1 0Y2 1R3 0Z2", "2R3 f0 0Y3 0Z3", "1Y1 1Z1 1Y2 f1",
    "0Y4 0Z4 2Y1 2Z1", "1Z2 2Y2 f2 0Y5", "1Y3 1Z3 2Z2 1Y4", "0Z5 0M 1Z4 2Y3", "2Z3 0D 1Y5 2Y4",
    "0G 0g0 1Z5 2Z4", "1M 0M1 0g1 2Y5", "1D 0D2 1G 1g0", "2Z5 2M 0M2 1M1", "1g1 0g2 2D 1D2",
    "2G 2g0 2M1 0D3", "0M3 1M2 2g1 2D2", "1g2 0g3 0D4 2M2", "0M4 1D3 1M3 2g2", "1D4 2M3 1g3 0g4",
    "2D3 1M4 2D4 2g3", "2M4 1g4 0F 2g4", "0g5 1F 1g5 2g5", "2F",
)


def kernel(
    anc_ref, pan_ref, idx_ref, off_ref, diag_ref,
    a_buf, at_buf, g_buf, i_own, i_buf, i_far, i_mix, part, q1r, q2s, q2r, s_row, s_col, member,
    d_half, m_half, d2s, d1r, d2r, d3s, d3r, d_pass, s_pass,
    mcr, m1s, m1r, m2s, m2r, m3s, m3r, mts, mtr,
    g_send, g_swap, g_half, g_recv, grow, gcol,
    send_sem, recv_sem, load_sem,
):
    row = lax.axis_index("row")
    col = lax.axis_index("col")
    core = lax.rem(row, 2)
    y = lax.rem(lax.div(row, 2), 4)
    x_lo = lax.div(row, 8)
    x_hi = lax.rem(col, 2)
    z = lax.div(col, 2)
    x = x_hi * 2 + x_lo
    where = {"x": x, "y": y, "z": z}
    y1, y2, y3 = mod(y + 1, 4), mod(y + 2, 4), mod(y + 3, 4)
    z1, z2, z3 = mod(z + 1, 4), mod(z + 2, 4), mod(z + 3, 4)

    def device(px, py, pz, pc):
        return (lax.rem(px, 2) * 8 + py * 2 + pc, pz * 2 + lax.div(px, 2))

    def neighbour(axis, step):
        place = dict(where)
        place[axis] = mod(place[axis] + step, 4)
        return device(place["x"], place["y"], place["z"], core)

    partner = (row + 1 - 2 * core, col)
    x_near = (row + 8 - 16 * x_lo, col)
    turned = lax.rem(col + z, 4)
    flip = lax.rem(x_hi + lax.div(z, 2), 2)
    turn_to = (2 * col + core, lax.rem(y + turned, 4) * 2 + lax.rem(x_lo + flip, 2))
    fixed = (turn_to[0] == row) & (turn_to[1] == col)
    lane = lax.broadcasted_iota(jnp.int32, (1, 128), 1)

    used = [0]
    copies = []

    def remote(src, dst, dev):
        n = used[0]
        used[0] += 1
        assert n < N_SEM
        copy = pltpu.make_async_remote_copy(
            src_ref=src, dst_ref=dst, send_sem=send_sem.at[n], recv_sem=recv_sem.at[n],
            device_id=dev, device_id_type=MESH,
        )
        copies.append(copy)
        return copy

    def send(src, dst, dev):
        copy = remote(src, dst, dev)
        copy.start()
        return copy

    orders = (("x", "y", "z"), ("y", "z", "x"), ("z", "x", "y"))
    loads = []
    for s, (ra, rb, rc) in enumerate(orders):
        loads.append(
            pltpu.make_async_copy(
                pan_ref.at[s], g_buf.at[s, where[rb], where[ra], core], load_sem.at[1 + s]
            )
        )
    load_i = pltpu.make_async_copy(idx_ref, i_own, load_sem.at[4])
    load_i.start()
    for one in loads:
        one.start()
    load_a = pltpu.make_async_copy(anc_ref, a_buf, load_sem.at[0])
    load_a.start()

    barrier = pltpu.get_barrier_semaphore()
    for axis in ("x", "y", "z"):
        for step in (1, 2, 3):
            pl.semaphore_signal(
                barrier, inc=1, device_id=neighbour(axis, step), device_id_type=MESH
            )
    pl.semaphore_signal(barrier, inc=1, device_id=partner, device_id_type=MESH)
    load_i.wait()
    lists = i_own[...]
    twice = jnp.concatenate([lists, lists], axis=1)
    for s, (ra, rb, rc) in enumerate(orders):
        i_buf[s, where[rb], where[ra], pl.ds(0, 3), :] = twice
        i_buf[s, where[rb], where[ra], pl.ds(3, 1), :] = twice[:1]
    for one in loads:
        one.wait()
    pl.semaphore_wait(barrier, 10)

    def gather(axis, whole, half):
        here = where[axis]
        plus, minus = neighbour(axis, 1), neighbour(axis, 3)
        before, after = mod(here + 3, 4), mod(here + 1, 4)
        up = send(whole(here), whole(here), plus)
        down = send(whole(here), whole(here), minus)
        yield
        up.wait_recv()
        up2 = send(half(before, 0), half(before, 0), plus)
        down.wait_recv()
        down2 = send(half(after, 1), half(after, 1), minus)
        yield
        up2.wait_recv()
        down2.wait_recv()
        yield

    def gather_short(axis, whole):
        here = where[axis]
        sent = [send(whole(here), whole(here), neighbour(axis, step)) for step in (1, 3, 2)]
        yield
        for one in sent:
            one.wait_recv()
        yield

    def run(*paths):
        for path in paths:
            next(path)

    across = {}

    def cross(key, ref):
        across[key] = send(ref, ref, partner)

    row_start = row * 1024
    col_start = col * 2048

    def mask(i, _):
        r0 = pl.multiple_of(i * 128, 128)
        val = a_buf[pl.ds(r0, 128), :].astype(F32)
        gap = (
            lax.broadcasted_iota(jnp.int32, (128, 2048), 1)
            - lax.broadcasted_iota(jnp.int32, (128, 2048), 0)
            + (col_start - row_start - i * 128)
        )
        a_buf[pl.ds(r0, 128), :] = jnp.where(gap <= 0, val, 0.0).astype(BF16)
        at_buf[:, pl.ds(r0, 128)] = jnp.where(gap < 0, val, 0.0).T.astype(BF16)
        return 0

    ring_a, ring_b, list_a, list_b, list_c = [], [], [], [], []
    for s, (ra, rb, rc) in enumerate(orders):
        g, own, mix, mb = g_buf.at[s], i_buf.at[s], i_mix.at[s], where[rb]
        ring_a.append(gather_short(ra, lambda i, g=g, mb=mb: g.at[mb, i, core]))
        ring_b.append(
            gather(rb, lambda i, g=g: g.at[i, :, core],
                   lambda i, h, g=g: g.at[i, pl.ds(2 * h, 2), core])
        )
        list_a.append(gather_short(ra, lambda i, own=own, mb=mb: own.at[mb, i]))
        list_b.append(gather_short(rb, lambda i, own=own: own.at[i]))
        list_c.append(gather_short(rc, lambda i, mix=mix: mix.at[i]))

    def cross_panels(s, step):
        j = mod(where[orders[s][1]] + step, 4)
        cross((s, "g", step), g_buf.at[s, j, :, core])

    run(*ring_a, *list_a)
    load_a.wait()
    lax.fori_loop(0, 4, mask, 0)
    for s in range(3):
        run(ring_a[s], ring_b[s])
    for s in range(3):
        run(list_a[s], list_b[s])
        cross_panels(s, 0)
    lax.fori_loop(4, 6, mask, 0)
    for s in range(3):
        run(ring_b[s])
    for s in range(3):
        cross_panels(s, 3)
        cross_panels(s, 1)
        run(list_b[s])
        across[s, "i"] = send(i_buf.at[s], i_far.at[s], partner)
    lax.fori_loop(6, 8, mask, 0)
    for s in range(3):
        run(ring_b[s])
        cross_panels(s, 2)
    for s in range(3):
        across[s, "i"].wait_recv()
        i_mix[s, where[orders[s][2]]] = jnp.where(
            (lane < 64) == (core == 0), i_buf[s], i_far[s]
        )
        run(list_c[s])

    level = lax.broadcasted_iota(jnp.int32, (128, 128), 0).astype(F32).astype(BF16)

    def spread_part(s):
        rc = orders[s][2]
        pieces = [
            i_mix[s, where[rc], cb, ca, pl.ds(s, 1), :] for cb in range(4) for ca in range(4)
        ]

        def block(i, _):
            place = dict(where)
            place[rc] = i
            to_row, to_col = device(place["x"], place["y"], place["z"], core)
            halves = []
            for base in (to_row * 1024 + to_col * 128, to_col * 2048 + to_row * 128):
                hots = []
                for piece in pieces:
                    rel = piece - base
                    rel = jnp.where((rel >= 0) & (rel < 128), rel, -1).astype(F32).astype(BF16)
                    hots.append(jnp.where(level == rel, jnp.ones((), BF16), jnp.zeros((), BF16)))
                halves.append(jnp.concatenate(hots, axis=1))
            out = jnp.dot(
                jnp.concatenate(halves, axis=0), g_buf[s].reshape(2048, 256),
                preferred_element_type=F32,
            )
            part[s, i] = out.astype(BF16).reshape(2, 128, 256)
            return 0

        lax.fori_loop(0, 4, block, 0)

    def mirrored(s):
        def tile(t, _):
            rows = pl.ds(pl.multiple_of(t * 1024, 1024), 1024)
            out = jnp.dot(
                at_buf[rows, :], s_row[s].reshape(1024, 256), preferred_element_type=F32
            )
            m_half[s, pl.ds(4 * t, 4)] = out.astype(BF16).reshape(4, 2, 128, 256)
            return 0

        lax.fori_loop(0, 2, tile, 0)

    def direct(s):
        def tile(t, _):
            rows = pl.ds(pl.multiple_of(t * 512, 512), 512)
            out = jnp.dot(
                a_buf[rows, :], s_col[s].reshape(2048, 256), preferred_element_type=F32
            )
            d_half[s, pl.ds(4 * t, 4)] = out.astype(BF16).reshape(4, 128, 256)
            return 0

        lax.fori_loop(0, 2, tile, 0)

    along = (((0,), (0,)), ((), ()))
    x_plus, x_minus = neighbour("x", 1), neighbour("x", 3)
    y_plus, y_minus = neighbour("y", 1), neighbour("y", 3)
    z_plus, z_minus = neighbour("z", 1), neighbour("z", 3)

    steps = {}

    def flow(names, path):
        for name in names:
            steps[name] = path

    turns = []

    def spread(s):
        axis = orders[s][2]
        here = where[axis]
        plus, minus = neighbour(axis, 1), neighbour(axis, 3)
        h1, h2, h3 = mod(here + 1, 4), mod(here + 2, 4), mod(here + 3, 4)
        for step in range(4):
            across[s, "g", step].wait_recv()
        spread_part(s)
        p1 = send(part.at[s, h2, 0], q1r.at[s, 0], plus)
        n1 = send(part.at[s, h2, 1], q1r.at[s, 1], minus)
        p2b = send(part.at[s, h1, 1], q2r.at[s, 0, 1], plus)
        n2a = send(part.at[s, h3, 0], q2r.at[s, 1, 0], minus)
        yield
        p1.wait_recv()
        q2s[s, 0] = part[s, h1, 0] + q1r[s, 0]
        p2a = send(q2s.at[s, 0], q2r.at[s, 0, 0], plus)
        n1.wait_recv()
        q2s[s, 1] = part[s, h3, 1] + q1r[s, 1]
        n2b = send(q2s.at[s, 1], q2r.at[s, 1, 1], minus)
        yield
        for one in (p2b, n2a, p2a, n2b):
            one.wait_recv()
        s_row[s, col] = part[s, here, 0] + q2r[s, 0, 0] + q2r[s, 1, 0]
        s_col[s, row] = part[s, here, 1] + q2r[s, 0, 1] + q2r[s, 1, 1]
        flow([f"{s}Y{n}" for n in range(1, 6)], column_rows(s))
        flow([f"{s}Z{n}" for n in range(1, 6)], row_rows(s))
        run(steps[f"{s}Y1"], steps[f"{s}Z1"])
        yield

    def opposite(src, passed, dst):
        plus, minus = neighbour("x", 1), neighbour("x", 3)
        first, last = pl.ds(0, 64), pl.ds(64, 64)
        up = send(src.at[first], passed.at[0], plus)
        down = send(src.at[last], passed.at[1], minus)
        yield
        up.wait_recv()
        up2 = send(passed.at[0], dst(3).at[first], plus)
        down.wait_recv()
        down2 = send(passed.at[1], dst(1).at[last], minus)
        yield
        up2.wait_recv()
        down2.wait_recv()
        yield

    def half_rows(ref):
        return lambda i, h: ref(i).at[pl.ds(64 * h, 64)]

    def column_rows(s):
        def slot(lo):
            return lambda i: s_col.at[s, lo * 8 + i * 2 + core]

        def cross_slot(name, lo, i):
            cross((s, name), slot(lo)(i))

        own = gather("y", slot(x_lo), half_rows(slot(x_lo)))
        far = gather("y", slot(1 - x_lo), half_rows(slot(1 - x_lo)))
        near = send(s_col.at[s, row], s_col.at[s, row], x_near)
        run(own)
        cross_slot("o0", x_lo, y)
        yield
        near.wait_recv()
        run(far)
        cross_slot("f0", 1 - x_lo, y)
        yield
        run(own)
        cross_slot("o3", x_lo, y3)
        cross_slot("o1", x_lo, y1)
        yield
        run(own)
        cross_slot("o2", x_lo, y2)
        yield
        run(far)
        cross_slot("f3", 1 - x_lo, y3)
        cross_slot("f1", 1 - x_lo, y1)
        yield
        run(far)
        cross_slot("f2", 1 - x_lo, y2)
        yield

    def row_rows(s):
        def slot(hi):
            return lambda i: s_row.at[s, i * 2 + hi]

        own = gather("z", slot(x_hi), half_rows(slot(x_hi)))
        far = gather("z", slot(1 - x_hi), half_rows(slot(1 - x_hi)))
        away = opposite(
            s_row.at[s, col], s_pass.at[s],
            lambda step: s_row.at[s, z * 2 + lax.div(mod(x + step, 4), 2)],
        )
        run(away)
        run(own)
        yield
        run(away)
        run(own)
        yield
        run(away)
        run(far)
        yield
        run(own)
        yield
        run(far)
        yield
        run(far)
        yield

    def mirrored_sum(s):
        mirrored(s)
        m0 = send(m_half.at[s, pl.ds(4 - 4 * core, 4)], mcr.at[s], partner)
        yield
        m0.wait_recv()

        def val(lo, i):
            n, hi = mod(i + turned, 4), lax.rem(lo + flip, 2)
            return m_half[s, core * 4 + n, hi].astype(F32) + mcr[s, n, hi].astype(F32)

        m1s[s, 0] = val(0, y2).astype(BF16)
        p1 = send(m1s.at[s, 0], m1r.at[s, 0], y_plus)
        m1s[s, 1] = val(1, y2).astype(BF16)
        n1 = send(m1s.at[s, 1], m1r.at[s, 1], y_minus)
        m2s[s, 0, 1] = val(1, y1).astype(BF16)
        p2b = send(m2s.at[s, 0, 1], m2r.at[s, 0, 1], y_plus)
        m2s[s, 1, 0] = val(0, y3).astype(BF16)
        n2a = send(m2s.at[s, 1, 0], m2r.at[s, 1, 0], y_minus)
        yield
        p1.wait_recv()
        m2s[s, 0, 0] = (val(0, y1) + m1r[s, 0].astype(F32)).astype(BF16)
        p2a = send(m2s.at[s, 0, 0], m2r.at[s, 0, 0], y_plus)
        n1.wait_recv()
        m2s[s, 1, 1] = (val(1, y3) + m1r[s, 1].astype(F32)).astype(BF16)
        n2b = send(m2s.at[s, 1, 1], m2r.at[s, 1, 1], y_minus)
        yield
        for one in (p2b, n2a, p2a, n2b):
            one.wait_recv()
        def total(lo):
            return val(lo, y) + m2r[s, 0, lo].astype(F32) + m2r[s, 1, lo].astype(F32)

        m3s[s] = total(1 - x_lo).astype(BF16)
        e = send(m3s.at[s], m3r.at[s], x_near)
        yield
        e.wait_recv()
        mts[s] = (total(x_lo) + m3r[s].astype(F32)).astype(BF16)
        turn = remote(mts.at[s], mtr.at[s], turn_to)

        @pl.when(jnp.logical_not(fixed))
        def _():
            turn.start()

        @pl.when(fixed)
        def _():
            mtr[s] = mts[s]

        turns.append(turn)
        yield

        @pl.when(jnp.logical_not(fixed))
        def _():
            turn.wait_recv()

        yield mtr[s].astype(F32)

    def direct_sum(s):
        for name in ("o0", "o3", "o1", "f0", "o2", "f3", "f1", "f2"):
            across[s, name].wait_recv()
        direct(s)
        p1 = send(d_half.at[s, z2 * 2], d1r.at[s, 0], z_plus)
        n1 = send(d_half.at[s, z2 * 2 + 1], d1r.at[s, 1], z_minus)
        p2b = send(d_half.at[s, z1 * 2 + 1], d2r.at[s, 0, 1], z_plus)
        n2a = send(d_half.at[s, z3 * 2], d2r.at[s, 1, 0], z_minus)
        yield
        p1.wait_recv()
        d2s[s, 0] = (d_half[s, z1 * 2].astype(F32) + d1r[s, 0].astype(F32)).astype(BF16)
        p2a = send(d2s.at[s, 0], d2r.at[s, 0, 0], z_plus)
        n1.wait_recv()
        d2s[s, 1] = (d_half[s, z3 * 2 + 1].astype(F32) + d1r[s, 1].astype(F32)).astype(BF16)
        n2b = send(d2s.at[s, 1], d2r.at[s, 1, 1], z_minus)
        yield
        for one in (p2b, n2a, p2a, n2b):
            one.wait_recv()

        def total(hi):
            return (
                d_half[s, z * 2 + hi].astype(F32)
                + d2r[s, 0, hi].astype(F32) + d2r[s, 1, hi].astype(F32)
            )

        d3s[s] = total(1 - x_hi).astype(BF16)
        away = opposite(d3s.at[s], d_pass.at[s], lambda step: d3r.at[s])
        run(away)
        yield
        run(away)
        yield
        run(away)
        yield total(x_hi) + d3r[s].astype(F32)

    def finish(s):
        product = next(steps[f"{s}M"]) + next(steps[f"{s}D"])
        off_ref[:, pl.ds(s * 256, 256)] = jnp.where(member[s] > 0.5, product, 0.0).astype(BF16)
        yield

    def share(s):
        out = lax.dot_general(
            s_row[s].reshape(1024, 256), d_half[s].reshape(1024, 256), along,
            preferred_element_type=F32,
        ) + lax.dot_general(
            s_col[s].reshape(2048, 256), m_half[s].reshape(2048, 256), along,
            preferred_element_type=F32,
        )
        g_send[s] = out.astype(BF16).reshape(8, 2, G_ROWS, 256)
        yield


    near = [(lax.rem(lax.div(row, 2) + n, 8)) for n in range(1, 8)]
    pair = lax.div(row, 2)

    def diagonal(s):
        swap = send(g_send.at[s, :, 1 - core], g_swap.at[s], partner)
        yield
        swap.wait_recv()
        g_half[s] = (g_send[s, :, core].astype(F32) + g_swap[s].astype(F32)).astype(BF16)
        sends = [
            send(g_half.at[s, n], g_recv.at[s, pair], (2 * n + core, col)) for n in near
        ]
        yield
        for one in sends:
            one.wait_recv()
        total = g_half[s, pair].astype(F32)
        for n in near:
            total = total + g_recv[s, n].astype(F32)
        grow[s, col] = total.astype(BF16)
        own = grow.at[s, col]
        sends = [send(own, own, (row, mod(col + step, 8))) for step in range(1, 8)]
        yield
        for one in sends:
            one.wait_recv()
        total = grow[s, 0].astype(F32)
        for n in range(1, 8):
            total = total + grow[s, n].astype(F32)
        own = gcol.at[s, pair, core]
        gcol[s, pair, core] = total.astype(BF16)
        sends = [send(own, own, (2 * n + core, col)) for n in near]
        yield
        for one in sends:
            one.wait_recv()
        swap = send(gcol.at[s, :, core], gcol.at[s, :, core], partner)
        yield
        swap.wait_recv()
        diag_ref[s] = gcol[s].astype(F32).reshape(256, 256)
        yield

    def flags(s):
        run(list_c[s])
        own_rows = lax.broadcasted_iota(jnp.int32, (128, 128), 0) + (row * 1024 + col * 128)

        def seen(n, found):
            pz, py = lax.div(n, 4), lax.rem(n, 4)
            for px in range(4):
                line = i_mix[s, pz, py, px, pl.ds(s, 1), :]
                found = jnp.where(own_rows == line, 1.0, found)
            return found

        found = lax.fori_loop(0, 16, seen, jnp.zeros((128, 128), F32))
        flag = jnp.max(found, axis=1, keepdims=True)
        member[s] = jnp.broadcast_to(flag, (128, 256))
        yield

    for s in range(3):
        flow([f"{s}P", f"{s}R2", f"{s}R3"], spread(s))
        flow([f"{s}M"] + [f"{s}M{n}" for n in range(1, 5)], mirrored_sum(s))
        flow([f"{s}D", f"{s}D2", f"{s}D3", f"{s}D4"], direct_sum(s))
        flow([f"{s}G"], share(s))
        flow([f"{s}F"], finish(s))
        flow([f"f{s}"], flags(s))
        flow([f"{s}g{n}" for n in range(6)], diagonal(s))
    for name in " ".join(ORDER).split():
        run(steps[name])

    for one in copies:
        if all(one is not turn for turn in turns):
            one.wait_send()

    @pl.when(jnp.logical_not(fixed))
    def _():
        for turn in turns:
            turn.wait_send()


def per_device(ancestor, panels, row_index, diag_inverse):
    V = pltpu.VMEM
    any_spec = pl.BlockSpec(memory_space=pltpu.HBM)
    vmem_spec = pl.BlockSpec(memory_space=pltpu.VMEM)
    piece = (128, 256)
    thin = (G_ROWS, 256)

    scratch = [
        V((1024, 2048), BF16), V((2048, 1024), BF16),
        V((3, 4, 4, 2, 64, 256), BF16),
        V((3, 64), jnp.int32), V((3, 4, 4, 4, 128), jnp.int32), V((3, 4, 4, 4, 128), jnp.int32),
        V((3, 4, 4, 4, 4, 128), jnp.int32),
        V((3, 4, 2, *piece), BF16), V((3, 2, *piece), BF16),
        V((3, 2, *piece), BF16), V((3, 2, 2, *piece), BF16),
        V((3, 8, *piece), BF16), V((3, 16, *piece), BF16), V((3, *piece), F32),
        V((3, 8, *piece), BF16), V((3, 8, 2, *piece), BF16),
        V((3, 2, *piece), BF16), V((3, 2, *piece), BF16), V((3, 2, 2, *piece), BF16),
        V((3, *piece), BF16), V((3, *piece), BF16), V((3, 2, 64, 256), BF16), V((3, 2, 64, 256), BF16),
        V((3, 4, 2, *piece), BF16),
        V((3, 2, *piece), BF16), V((3, 2, *piece), BF16),
        V((3, 2, 2, *piece), BF16), V((3, 2, 2, *piece), BF16),
        V((3, *piece), BF16), V((3, *piece), BF16), V((3, *piece), BF16), V((3, *piece), BF16),
        V((3, 8, 2, *thin), BF16), V((3, 8, *thin), BF16), V((3, 8, *thin), BF16),
        V((3, 8, *thin), BF16), V((3, 8, *thin), BF16), V((3, 8, 2, *thin), BF16),
        pltpu.SemaphoreType.DMA((N_SEM,)), pltpu.SemaphoreType.DMA((N_SEM,)),
        pltpu.SemaphoreType.DMA((5,)),
    ]
    ancestor = pltpu.with_memory_space_constraint(ancestor, pltpu.HBM)
    panels = pltpu.with_memory_space_constraint(panels, pltpu.HBM)
    row_index = pltpu.with_memory_space_constraint(row_index, pltpu.HBM)
    kept, blocks = pl.pallas_call(
        kernel,
        out_shape=(
            jax.ShapeDtypeStruct((128, 768), BF16),
            jax.ShapeDtypeStruct((3, 256, 256), F32),
        ),
        in_specs=[any_spec, any_spec, any_spec],
        out_specs=(vmem_spec, vmem_spec),
        scratch_shapes=scratch,
        compiler_params=pltpu.CompilerParams(
            collective_id=0, has_side_effects=True, vmem_limit_bytes=48 * 2**20
        ),
        name="selected_inverse",
    )(ancestor, panels, row_index)
    return 0 - kept, diag_inverse + blocks


def solution(mesh):
    in_specs = (P("row", "col"), P(None, ("row", "col"), None), P(None, ("row", "col")), P())
    out_specs = (P(("row", "col"), None), P())
    return jax.shard_map(
        per_device, mesh=mesh, in_specs=in_specs, out_specs=out_specs, check_vma=False
    )
```

```python
import jax
import jax.numpy as jnp
from jax import lax
from jax.experimental import pallas as pl
from jax.experimental.pallas import tpu as pltpu
from jax.sharding import PartitionSpec as P

MESH = pl.DeviceIdType.MESH
F32 = jnp.float32
BF16 = jnp.bfloat16
N_SEM = 336
G_ROWS = 16


def mod(value, size):
    return lax.rem(value + 2 * size, size)


ORDER = (
    "0P 1P 0R2 2P", "1R2 0R3 2R2 0Y1", "0Z1 0Y2 1R3 0Z2", "2R3 f0 0Y3 0Z3", "1Y1 1Z1 1Y2 f1",
    "0Y4 0Z4 2Y1 2Z1", "1Z2 2Y2 f2 0Y5", "1Y3 1Z3 2Z2 1Y4", "0Z5 0M 1Z4 2Y3", "2Z3 0D 1Y5 2Y4",
    "0G 0g0 1Z5 2Z4", "1M 0M1 0g1 2Y5", "1D 0D2 1G 1g0", "2Z5 2M 0M2 1M1", "1g1 0g2 2D 1D2",
    "2M1 2G 2g0 0D3", "0M3 1M2 2g1 2D2", "1g2 0g3 0D4 2M2", "0M4 1D3 1M3 2g2", "1D4 2M3 1g3 0g4",
    "2D3 2M4 1M4 2D4", "2g3 1g4 0F 2g4", "0g5 1F 1g5 2g5", "2F",
)


def kernel(
    anc_ref, pan_ref, idx_ref, off_ref, diag_ref,
    a_buf, at_buf, g_buf, i_own, i_buf, i_far, i_mix, part, q1r, q2s, q2r, s_row, s_col, member,
    d_half, m_half, d2s, d1r, d2r, d3s, d3r, d_pass, s_pass,
    mcr, m1s, m1r, m2s, m2r, m3s, m3r, mts, mtr,
    g_send, g_swap, g_half, g_recv, grow, gcol,
    send_sem, recv_sem, load_sem,
):
    row = lax.axis_index("row")
    col = lax.axis_index("col")
    core = lax.rem(row, 2)
    y = lax.rem(lax.div(row, 2), 4)
    x_lo = lax.div(row, 8)
    x_hi = lax.rem(col, 2)
    z = lax.div(col, 2)
    x = x_hi * 2 + x_lo
    where = {"x": x, "y": y, "z": z}
    y1, y2, y3 = mod(y + 1, 4), mod(y + 2, 4), mod(y + 3, 4)
    z1, z2, z3 = mod(z + 1, 4), mod(z + 2, 4), mod(z + 3, 4)

    def device(px, py, pz, pc):
        return (lax.rem(px, 2) * 8 + py * 2 + pc, pz * 2 + lax.div(px, 2))

    def neighbour(axis, step):
        place = dict(where)
        place[axis] = mod(place[axis] + step, 4)
        return device(place["x"], place["y"], place["z"], core)

    partner = (row + 1 - 2 * core, col)
    x_near = (row + 8 - 16 * x_lo, col)
    turned = lax.rem(col + z, 4)
    flip = lax.rem(x_hi + lax.div(z, 2), 2)
    turn_to = (2 * col + core, lax.rem(y + turned, 4) * 2 + lax.rem(x_lo + flip, 2))
    fixed = (turn_to[0] == row) & (turn_to[1] == col)
    lane = lax.broadcasted_iota(jnp.int32, (1, 128), 1)

    used = [0]
    copies = []

    def remote(src, dst, dev):
        n = used[0]
        used[0] += 1
        assert n < N_SEM
        copy = pltpu.make_async_remote_copy(
            src_ref=src, dst_ref=dst, send_sem=send_sem.at[n], recv_sem=recv_sem.at[n],
            device_id=dev, device_id_type=MESH,
        )
        copies.append(copy)
        return copy

    def send(src, dst, dev):
        copy = remote(src, dst, dev)
        copy.start()
        return copy

    orders = (("x", "y", "z"), ("y", "z", "x"), ("z", "x", "y"))
    loads = []
    for s, (ra, rb, rc) in enumerate(orders):
        loads.append(
            pltpu.make_async_copy(
                pan_ref.at[s], g_buf.at[s, where[rb], where[ra], core], load_sem.at[1 + s]
            )
        )
    load_i = pltpu.make_async_copy(idx_ref, i_own, load_sem.at[4])
    load_i.start()
    for one in loads:
        one.start()
    load_a = pltpu.make_async_copy(anc_ref, a_buf, load_sem.at[0])
    load_a.start()

    barrier = pltpu.get_barrier_semaphore()
    for axis in ("x", "y", "z"):
        for step in (1, 2, 3):
            pl.semaphore_signal(
                barrier, inc=1, device_id=neighbour(axis, step), device_id_type=MESH
            )
    pl.semaphore_signal(barrier, inc=1, device_id=partner, device_id_type=MESH)
    load_i.wait()
    lists = i_own[...]
    twice = jnp.concatenate([lists, lists], axis=1)
    for s, (ra, rb, rc) in enumerate(orders):
        i_buf[s, where[rb], where[ra], pl.ds(0, 3), :] = twice
        i_buf[s, where[rb], where[ra], pl.ds(3, 1), :] = twice[:1]
    for one in loads:
        one.wait()
    pl.semaphore_wait(barrier, 10)

    def gather(axis, whole, half):
        here = where[axis]
        plus, minus = neighbour(axis, 1), neighbour(axis, 3)
        before, after = mod(here + 3, 4), mod(here + 1, 4)
        up = send(whole(here), whole(here), plus)
        down = send(whole(here), whole(here), minus)
        yield
        up.wait_recv()
        up2 = send(half(before, 0), half(before, 0), plus)
        down.wait_recv()
        down2 = send(half(after, 1), half(after, 1), minus)
        yield
        up2.wait_recv()
        down2.wait_recv()
        yield

    def gather_short(axis, whole):
        here = where[axis]
        sent = [send(whole(here), whole(here), neighbour(axis, step)) for step in (1, 3, 2)]
        yield
        for one in sent:
            one.wait_recv()
        yield

    def run(*paths):
        for path in paths:
            next(path)

    across = {}

    def cross(key, ref):
        across[key] = send(ref, ref, partner)

    row_start = row * 1024
    col_start = col * 2048

    def mask(i, _):
        r0 = pl.multiple_of(i * 128, 128)
        val = a_buf[pl.ds(r0, 128), :].astype(F32)
        gap = (
            lax.broadcasted_iota(jnp.int32, (128, 2048), 1)
            - lax.broadcasted_iota(jnp.int32, (128, 2048), 0)
            + (col_start - row_start - i * 128)
        )
        a_buf[pl.ds(r0, 128), :] = jnp.where(gap <= 0, val, 0.0).astype(BF16)
        at_buf[:, pl.ds(r0, 128)] = jnp.where(gap < 0, val, 0.0).T.astype(BF16)
        return 0

    ring_a, ring_b, list_a, list_b, list_c = [], [], [], [], []
    for s, (ra, rb, rc) in enumerate(orders):
        g, own, mix, mb = g_buf.at[s], i_buf.at[s], i_mix.at[s], where[rb]
        ring_a.append(gather_short(ra, lambda i, g=g, mb=mb: g.at[mb, i, core]))
        ring_b.append(
            gather(rb, lambda i, g=g: g.at[i, :, core],
                   lambda i, h, g=g: g.at[i, pl.ds(2 * h, 2), core])
        )
        list_a.append(gather_short(ra, lambda i, own=own, mb=mb: own.at[mb, i]))
        list_b.append(gather_short(rb, lambda i, own=own: own.at[i]))
        list_c.append(gather_short(rc, lambda i, mix=mix: mix.at[i]))

    def cross_panels(s, step):
        j = mod(where[orders[s][1]] + step, 4)
        cross((s, "g", step), g_buf.at[s, j, :, core])

    run(*ring_a, *list_a)
    load_a.wait()
    lax.fori_loop(0, 4, mask, 0)
    for s in range(3):
        run(ring_a[s], ring_b[s])
    for s in range(3):
        run(list_a[s], list_b[s])
        cross_panels(s, 0)
    lax.fori_loop(4, 6, mask, 0)
    for s in range(3):
        run(ring_b[s])
    for s in range(3):
        cross_panels(s, 3)
        cross_panels(s, 1)
        run(list_b[s])
        across[s, "i"] = send(i_buf.at[s], i_far.at[s], partner)
    lax.fori_loop(6, 8, mask, 0)
    for s in range(3):
        run(ring_b[s])
        cross_panels(s, 2)
    for s in range(3):
        across[s, "i"].wait_recv()
        i_mix[s, where[orders[s][2]]] = jnp.where(
            (lane < 64) == (core == 0), i_buf[s], i_far[s]
        )
        run(list_c[s])

    level = lax.broadcasted_iota(jnp.int32, (128, 128), 0).astype(F32).astype(BF16)

    def spread_part(s):
        rc = orders[s][2]
        pieces = [
            i_mix[s, where[rc], cb, ca, pl.ds(s, 1), :] for cb in range(4) for ca in range(4)
        ]

        def block(i, _):
            place = dict(where)
            place[rc] = i
            to_row, to_col = device(place["x"], place["y"], place["z"], core)
            halves = []
            for base in (to_row * 1024 + to_col * 128, to_col * 2048 + to_row * 128):
                hots = []
                for piece in pieces:
                    rel = piece - base
                    rel = jnp.where((rel >= 0) & (rel < 128), rel, -1).astype(F32).astype(BF16)
                    hots.append(jnp.where(level == rel, jnp.ones((), BF16), jnp.zeros((), BF16)))
                halves.append(jnp.concatenate(hots, axis=1))
            out = jnp.dot(
                jnp.concatenate(halves, axis=0), g_buf[s].reshape(2048, 256),
                preferred_element_type=F32,
            )
            part[s, i] = out.astype(BF16).reshape(2, 128, 256)
            return 0

        lax.fori_loop(0, 4, block, 0)

    def mirrored(s):
        def tile(t, _):
            rows = pl.ds(pl.multiple_of(t * 1024, 1024), 1024)
            out = jnp.dot(
                at_buf[rows, :], s_row[s].reshape(1024, 256), preferred_element_type=F32
            )
            m_half[s, pl.ds(4 * t, 4)] = out.astype(BF16).reshape(4, 2, 128, 256)
            return 0

        lax.fori_loop(0, 2, tile, 0)

    def direct(s):
        def tile(t, _):
            rows = pl.ds(pl.multiple_of(t * 512, 512), 512)
            out = jnp.dot(
                a_buf[rows, :], s_col[s].reshape(2048, 256), preferred_element_type=F32
            )
            d_half[s, pl.ds(4 * t, 4)] = out.astype(BF16).reshape(4, 128, 256)
            return 0

        lax.fori_loop(0, 2, tile, 0)

    along = (((0,), (0,)), ((), ()))
    x_plus, x_minus = neighbour("x", 1), neighbour("x", 3)
    y_plus, y_minus = neighbour("y", 1), neighbour("y", 3)
    z_plus, z_minus = neighbour("z", 1), neighbour("z", 3)

    steps = {}

    def flow(names, path):
        for name in names:
            steps[name] = path

    turns = []

    def spread(s):
        axis = orders[s][2]
        here = where[axis]
        plus, minus = neighbour(axis, 1), neighbour(axis, 3)
        h1, h2, h3 = mod(here + 1, 4), mod(here + 2, 4), mod(here + 3, 4)
        for step in range(4):
            across[s, "g", step].wait_recv()
        spread_part(s)
        p1 = send(part.at[s, h2, 0], q1r.at[s, 0], plus)
        n1 = send(part.at[s, h2, 1], q1r.at[s, 1], minus)
        p2b = send(part.at[s, h1, 1], q2r.at[s, 0, 1], plus)
        n2a = send(part.at[s, h3, 0], q2r.at[s, 1, 0], minus)
        yield
        p1.wait_recv()
        q2s[s, 0] = part[s, h1, 0] + q1r[s, 0]
        p2a = send(q2s.at[s, 0], q2r.at[s, 0, 0], plus)
        n1.wait_recv()
        q2s[s, 1] = part[s, h3, 1] + q1r[s, 1]
        n2b = send(q2s.at[s, 1], q2r.at[s, 1, 1], minus)
        yield
        for one in (p2b, n2a, p2a, n2b):
            one.wait_recv()
        s_row[s, col] = part[s, here, 0] + q2r[s, 0, 0] + q2r[s, 1, 0]
        s_col[s, row] = part[s, here, 1] + q2r[s, 0, 1] + q2r[s, 1, 1]
        flow([f"{s}Y{n}" for n in range(1, 6)], column_rows(s))
        flow([f"{s}Z{n}" for n in range(1, 6)], row_rows(s))
        run(steps[f"{s}Y1"], steps[f"{s}Z1"])
        yield

    def opposite(src, passed, dst):
        plus, minus = neighbour("x", 1), neighbour("x", 3)
        first, last = pl.ds(0, 64), pl.ds(64, 64)
        up = send(src.at[first], passed.at[0], plus)
        down = send(src.at[last], passed.at[1], minus)
        yield
        up.wait_recv()
        up2 = send(passed.at[0], dst(3).at[first], plus)
        down.wait_recv()
        down2 = send(passed.at[1], dst(1).at[last], minus)
        yield
        up2.wait_recv()
        down2.wait_recv()
        yield

    def half_rows(ref):
        return lambda i, h: ref(i).at[pl.ds(64 * h, 64)]

    def column_rows(s):
        def slot(lo):
            return lambda i: s_col.at[s, lo * 8 + i * 2 + core]

        def cross_slot(name, lo, i):
            cross((s, name), slot(lo)(i))

        own = gather("y", slot(x_lo), half_rows(slot(x_lo)))
        far = gather("y", slot(1 - x_lo), half_rows(slot(1 - x_lo)))
        near = send(s_col.at[s, row], s_col.at[s, row], x_near)
        run(own)
        cross_slot("o0", x_lo, y)
        yield
        near.wait_recv()
        run(far)
        cross_slot("f0", 1 - x_lo, y)
        yield
        run(own)
        cross_slot("o3", x_lo, y3)
        cross_slot("o1", x_lo, y1)
        yield
        run(own)
        cross_slot("o2", x_lo, y2)
        yield
        run(far)
        cross_slot("f3", 1 - x_lo, y3)
        cross_slot("f1", 1 - x_lo, y1)
        yield
        run(far)
        cross_slot("f2", 1 - x_lo, y2)
        yield

    def row_rows(s):
        def slot(hi):
            return lambda i: s_row.at[s, i * 2 + hi]

        own = gather("z", slot(x_hi), half_rows(slot(x_hi)))
        far = gather("z", slot(1 - x_hi), half_rows(slot(1 - x_hi)))
        away = opposite(
            s_row.at[s, col], s_pass.at[s],
            lambda step: s_row.at[s, z * 2 + lax.div(mod(x + step, 4), 2)],
        )
        run(away)
        run(own)
        yield
        run(away)
        run(own)
        yield
        run(away)
        run(far)
        yield
        run(own)
        yield
        run(far)
        yield
        run(far)
        yield

    def mirrored_sum(s):
        mirrored(s)
        m0 = send(m_half.at[s, pl.ds(4 - 4 * core, 4)], mcr.at[s], partner)
        yield
        m0.wait_recv()

        def val(lo, i):
            n, hi = mod(i + turned, 4), lax.rem(lo + flip, 2)
            return m_half[s, core * 4 + n, hi].astype(F32) + mcr[s, n, hi].astype(F32)

        m1s[s, 0] = val(0, y2).astype(BF16)
        p1 = send(m1s.at[s, 0], m1r.at[s, 0], y_plus)
        m1s[s, 1] = val(1, y2).astype(BF16)
        n1 = send(m1s.at[s, 1], m1r.at[s, 1], y_minus)
        m2s[s, 0, 1] = val(1, y1).astype(BF16)
        p2b = send(m2s.at[s, 0, 1], m2r.at[s, 0, 1], y_plus)
        m2s[s, 1, 0] = val(0, y3).astype(BF16)
        n2a = send(m2s.at[s, 1, 0], m2r.at[s, 1, 0], y_minus)
        yield
        p1.wait_recv()
        m2s[s, 0, 0] = (val(0, y1) + m1r[s, 0].astype(F32)).astype(BF16)
        p2a = send(m2s.at[s, 0, 0], m2r.at[s, 0, 0], y_plus)
        n1.wait_recv()
        m2s[s, 1, 1] = (val(1, y3) + m1r[s, 1].astype(F32)).astype(BF16)
        n2b = send(m2s.at[s, 1, 1], m2r.at[s, 1, 1], y_minus)
        yield
        for one in (p2b, n2a, p2a, n2b):
            one.wait_recv()
        def total(lo):
            return val(lo, y) + m2r[s, 0, lo].astype(F32) + m2r[s, 1, lo].astype(F32)

        m3s[s] = total(1 - x_lo).astype(BF16)
        e = send(m3s.at[s], m3r.at[s], x_near)
        yield
        e.wait_recv()
        mts[s] = (total(x_lo) + m3r[s].astype(F32)).astype(BF16)
        turn = remote(mts.at[s], mtr.at[s], turn_to)

        @pl.when(jnp.logical_not(fixed))
        def _():
            turn.start()

        @pl.when(fixed)
        def _():
            mtr[s] = mts[s]

        turns.append(turn)
        yield

        @pl.when(jnp.logical_not(fixed))
        def _():
            turn.wait_recv()

        yield mtr[s].astype(F32)

    def direct_sum(s):
        for name in ("o0", "o3", "o1", "f0", "o2", "f3", "f1", "f2"):
            across[s, name].wait_recv()
        direct(s)
        p1 = send(d_half.at[s, z2 * 2], d1r.at[s, 0], z_plus)
        n1 = send(d_half.at[s, z2 * 2 + 1], d1r.at[s, 1], z_minus)
        p2b = send(d_half.at[s, z1 * 2 + 1], d2r.at[s, 0, 1], z_plus)
        n2a = send(d_half.at[s, z3 * 2], d2r.at[s, 1, 0], z_minus)
        yield
        p1.wait_recv()
        d2s[s, 0] = (d_half[s, z1 * 2].astype(F32) + d1r[s, 0].astype(F32)).astype(BF16)
        p2a = send(d2s.at[s, 0], d2r.at[s, 0, 0], z_plus)
        n1.wait_recv()
        d2s[s, 1] = (d_half[s, z3 * 2 + 1].astype(F32) + d1r[s, 1].astype(F32)).astype(BF16)
        n2b = send(d2s.at[s, 1], d2r.at[s, 1, 1], z_minus)
        yield
        for one in (p2b, n2a, p2a, n2b):
            one.wait_recv()

        def total(hi):
            return (
                d_half[s, z * 2 + hi].astype(F32)
                + d2r[s, 0, hi].astype(F32) + d2r[s, 1, hi].astype(F32)
            )

        d3s[s] = total(1 - x_hi).astype(BF16)
        away = opposite(d3s.at[s], d_pass.at[s], lambda step: d3r.at[s])
        run(away)
        yield
        run(away)
        yield
        run(away)
        yield total(x_hi) + d3r[s].astype(F32)

    def finish(s):
        product = next(steps[f"{s}M"]) + next(steps[f"{s}D"])
        off_ref[:, pl.ds(s * 256, 256)] = jnp.where(member[s] > 0.5, product, 0.0).astype(BF16)
        yield

    def share(s):
        out = lax.dot_general(
            s_row[s].reshape(1024, 256), d_half[s].reshape(1024, 256), along,
            preferred_element_type=F32,
        ) + lax.dot_general(
            s_col[s].reshape(2048, 256), m_half[s].reshape(2048, 256), along,
            preferred_element_type=F32,
        )
        g_send[s] = out.astype(BF16).reshape(8, 2, G_ROWS, 256)
        yield


    near = [(lax.rem(lax.div(row, 2) + n, 8)) for n in range(1, 8)]
    pair = lax.div(row, 2)

    def diagonal(s):
        swap = send(g_send.at[s, :, 1 - core], g_swap.at[s], partner)
        yield
        swap.wait_recv()
        g_half[s] = (g_send[s, :, core].astype(F32) + g_swap[s].astype(F32)).astype(BF16)
        sends = [
            send(g_half.at[s, n], g_recv.at[s, pair], (2 * n + core, col)) for n in near
        ]
        yield
        for one in sends:
            one.wait_recv()
        total = g_half[s, pair].astype(F32)
        for n in near:
            total = total + g_recv[s, n].astype(F32)
        grow[s, col] = total.astype(BF16)
        own = grow.at[s, col]
        sends = [send(own, own, (row, mod(col + step, 8))) for step in range(1, 8)]
        yield
        for one in sends:
            one.wait_recv()
        total = grow[s, 0].astype(F32)
        for n in range(1, 8):
            total = total + grow[s, n].astype(F32)
        own = gcol.at[s, pair, core]
        gcol[s, pair, core] = total.astype(BF16)
        sends = [send(own, own, (2 * n + core, col)) for n in near]
        yield
        for one in sends:
            one.wait_recv()
        swap = send(gcol.at[s, :, core], gcol.at[s, :, core], partner)
        yield
        swap.wait_recv()
        diag_ref[s] = gcol[s].astype(F32).reshape(256, 256)
        yield

    def flags(s):
        run(list_c[s])
        own_rows = lax.broadcasted_iota(jnp.int32, (128, 128), 0) + (row * 1024 + col * 128)

        def seen(n, found):
            pz, py = lax.div(n, 4), lax.rem(n, 4)
            for px in range(4):
                line = i_mix[s, pz, py, px, pl.ds(s, 1), :]
                found = jnp.where(own_rows == line, 1.0, found)
            return found

        found = lax.fori_loop(0, 16, seen, jnp.zeros((128, 128), F32))
        flag = jnp.max(found, axis=1, keepdims=True)
        member[s] = jnp.broadcast_to(flag, (128, 256))
        yield

    for s in range(3):
        flow([f"{s}P", f"{s}R2", f"{s}R3"], spread(s))
        flow([f"{s}M"] + [f"{s}M{n}" for n in range(1, 5)], mirrored_sum(s))
        flow([f"{s}D", f"{s}D2", f"{s}D3", f"{s}D4"], direct_sum(s))
        flow([f"{s}G"], share(s))
        flow([f"{s}F"], finish(s))
        flow([f"f{s}"], flags(s))
        flow([f"{s}g{n}" for n in range(6)], diagonal(s))
    for name in " ".join(ORDER).split():
        run(steps[name])

    for one in copies:
        if all(one is not turn for turn in turns):
            one.wait_send()

    @pl.when(jnp.logical_not(fixed))
    def _():
        for turn in turns:
            turn.wait_send()


def per_device(ancestor, panels, row_index, diag_inverse):
    V = pltpu.VMEM
    any_spec = pl.BlockSpec(memory_space=pltpu.HBM)
    vmem_spec = pl.BlockSpec(memory_space=pltpu.VMEM)
    piece = (128, 256)
    thin = (G_ROWS, 256)

    scratch = [
        V((1024, 2048), BF16), V((2048, 1024), BF16),
        V((3, 4, 4, 2, 64, 256), BF16),
        V((3, 64), jnp.int32), V((3, 4, 4, 4, 128), jnp.int32), V((3, 4, 4, 4, 128), jnp.int32),
        V((3, 4, 4, 4, 4, 128), jnp.int32),
        V((3, 4, 2, *piece), BF16), V((3, 2, *piece), BF16),
        V((3, 2, *piece), BF16), V((3, 2, 2, *piece), BF16),
        V((3, 8, *piece), BF16), V((3, 16, *piece), BF16), V((3, *piece), F32),
        V((3, 8, *piece), BF16), V((3, 8, 2, *piece), BF16),
        V((3, 2, *piece), BF16), V((3, 2, *piece), BF16), V((3, 2, 2, *piece), BF16),
        V((3, *piece), BF16), V((3, *piece), BF16), V((3, 2, 64, 256), BF16), V((3, 2, 64, 256), BF16),
        V((3, 4, 2, *piece), BF16),
        V((3, 2, *piece), BF16), V((3, 2, *piece), BF16),
        V((3, 2, 2, *piece), BF16), V((3, 2, 2, *piece), BF16),
        V((3, *piece), BF16), V((3, *piece), BF16), V((3, *piece), BF16), V((3, *piece), BF16),
        V((3, 8, 2, *thin), BF16), V((3, 8, *thin), BF16), V((3, 8, *thin), BF16),
        V((3, 8, *thin), BF16), V((3, 8, *thin), BF16), V((3, 8, 2, *thin), BF16),
        pltpu.SemaphoreType.DMA((N_SEM,)), pltpu.SemaphoreType.DMA((N_SEM,)),
        pltpu.SemaphoreType.DMA((5,)),
    ]
    ancestor = pltpu.with_memory_space_constraint(ancestor, pltpu.HBM)
    panels = pltpu.with_memory_space_constraint(panels, pltpu.HBM)
    row_index = pltpu.with_memory_space_constraint(row_index, pltpu.HBM)
    kept, blocks = pl.pallas_call(
        kernel,
        out_shape=(
            jax.ShapeDtypeStruct((128, 768), BF16),
            jax.ShapeDtypeStruct((3, 256, 256), F32),
        ),
        in_specs=[any_spec, any_spec, any_spec],
        out_specs=(vmem_spec, vmem_spec),
        scratch_shapes=scratch,
        compiler_params=pltpu.CompilerParams(
            collective_id=0, has_side_effects=True, vmem_limit_bytes=48 * 2**20
        ),
        name="selected_inverse",
    )(ancestor, panels, row_index)
    return 0 - kept, diag_inverse + blocks


def solution(mesh):
    in_specs = (P("row", "col"), P(None, ("row", "col"), None), P(None, ("row", "col")), P())
    out_specs = (P(("row", "col"), None), P())
    return jax.shard_map(
        per_device, mesh=mesh, in_specs=in_specs, out_specs=out_specs, check_vma=False
    )
```
